32 devices in a mesh: section: 2 (over core), tp: 4 (over z), mem: 4 (over y, x).
Axes of the slice: x: 2, y: 2, z: 4, core: 2. Of those that a mesh axis runs over, the one named last changes fastest.
Arguments:
- hidden_in: bfloat16 [8, 8192], P(None, 'mem'), may hold values from -12 to 12
- lengths: int32 [8], replicated, may hold values from 1 to 4096, as said below
- owner_order: int32 [8], replicated, may hold values from 0 to 7, each once
- attn_gain: bfloat16 [2, 8192], P('section', 'mem'), may hold values from 0.25 to 1.75
- w_query: bfloat16 [2, 8192, 8192], P('section', 'mem', 'tp'), may hold values from -0.0625 to 0.0625
- w_key: bfloat16 [2, 8192, 1024], P('section', 'mem', 'tp'), may hold values from -0.0625 to 0.0625
- w_value: bfloat16 [2, 8192, 1024], P('section', 'mem', 'tp'), may hold values from -0.0625 to 0.0625
- w_out: bfloat16 [2, 8192, 8192], P('section', 'tp', 'mem'), may hold values from -0.0625 to 0.0625
- ffn_gain: bfloat16 [2, 8192], P('section', 'mem'), may hold values from 0.25 to 1.75
- w_gate: bfloat16 [2, 8192, 14336], P('section', 'mem', 'tp'), may hold values from -0.0625 to 0.0625
- w_up: bfloat16 [2, 8192, 14336], P('section', 'mem', 'tp'), may hold values from -0.0625 to 0.0625
- w_down: bfloat16 [2, 14336, 8192], P('section', 'tp', 'mem'), may hold values from -0.046875 to 0.046875
- key_cache: bfloat16 [2, 8, 4096, 1024], P('section', 'mem', None, 'tp'), may hold values from -250 to 250
- value_cache: bfloat16 [2, 8, 4096, 1024], P('section', 'mem', None, 'tp'), may hold values from -12 to 12
Outputs:
- layer_outputs: bfloat16 [2, 8, 8192], P('section', None, 'mem')
The draws below stay inside these ranges and needn't reach their ends.
Inputs may be any that keep to these rules, and one draw needn't show every extreme that they name: Request r has lengths[r] filled positions in its cache; the largest length is exactly 4096. Cache slot j holds request owner_order[j]; index m of mem holds slots m * 2 to (m + 1) * 2 - 1.
All inputs are finite; a program needn't handle non-finite values.
Results may differ from the reference program's by a relative error of at most 0.014.
Values may be sent and summed in bfloat16 or wider, within the bound.
No kernel may reach another device: no remote copies, remote signals or barrier semaphores. Data moves between devices by JAX's collectives and lax.ppermute only.
A program may use at most 128 MiB of HBM per device.

```python
import math
import jax
import jax.numpy as jnp
from jax import lax

D = 8192
HQ = 64
KVH = 8
HD = 128
FF = 14336
CTX = 4096
BATCH = 8
LAYERS = 2


def draw_hidden_in(key, part):
    first = jax.random.fold_in(key, 0)
    base = jax.random.normal(first, (BATCH, D), jnp.float32)
    ramp = 0.5 * 3.0 ** (jnp.arange(D, dtype=jnp.float32) / D)
    values = base * ramp[None, :]
    return jnp.clip(values, -12.0, 12.0).astype(jnp.bfloat16)


def draw_lengths(key, part):
    first, second, third = jax.random.split(key, 3)
    levels = max(int(math.log2(CTX)), 1)
    powers = jax.random.randint(first, (BATCH,), 0, levels)
    lowest = jnp.left_shift(jnp.ones((BATCH,), jnp.int32), powers)
    extra = jax.random.randint(second, (BATCH,), 0, CTX)
    drawn = lowest + extra % lowest
    longest = jax.random.randint(third, (), 0, BATCH)
    return jnp.where(jnp.arange(BATCH) == longest, CTX, jnp.minimum(drawn, CTX)).astype(jnp.int32)


def draw_key_cache(key, part):
    first = jax.random.fold_in(key, 0)
    shape = (LAYERS, BATCH, CTX, KVH * HD)
    base = jnp.clip(jax.random.normal(first, shape, jnp.float32), -6.0, 6.0)
    values = base
    return values.astype(jnp.bfloat16)


def draw_value_cache(key, part):
    first, second = jax.random.split(key, 2)
    shape = (LAYERS, BATCH, CTX, KVH * HD)
    level = jax.random.normal(first, (LAYERS, BATCH, 1, KVH * HD), jnp.float32)
    values = level + 2.0 * jnp.clip(jax.random.normal(second, shape, jnp.float32), -4.5, 4.5)
    return jnp.clip(values, -12.0, 12.0).astype(jnp.bfloat16)


def shard_levels(stream_key, shape, pieces, low, high):
    def one(dim, blocks):
        heights = jax.random.uniform(jax.random.fold_in(jax.random.fold_in(stream_key, 6), dim), (blocks,), jnp.float32, low / len(pieces), high / len(pieces))
        return jnp.repeat(jnp.exp(heights), shape[dim] // blocks).reshape((-1,) + (1,) * (len(shape) - dim - 1))

    factor_of = one(*pieces[0])
    for cut in pieces[1:]:
        factor_of = factor_of * one(*cut)
    return factor_of


def scatter_about(stream_key, extent, width, reach, pieces=(), held_as=jnp.bfloat16):
    factor_of = shard_levels(stream_key, extent, pieces, -0.22, 0.18) if pieces else 1.0
    values = jax.random.normal(stream_key, extent, jnp.float32) * width * factor_of
    return jnp.minimum(jnp.maximum(values, -reach), reach).astype(held_as)


def setup_inputs(seed: int = 0) -> dict:
    arg_keys = jax.random.split(jax.random.key(seed), 15)
    hidden_in = draw_hidden_in(jax.random.fold_in(arg_keys[14], 71), 0)
    lengths = draw_lengths(jax.random.fold_in(arg_keys[14], 71), 0)
    owner_order = jax.random.permutation(arg_keys[2], BATCH).astype(jnp.int32)
    attn_gain = jnp.clip(1.0 + 0.15 * jax.random.normal(arg_keys[3], (LAYERS, D), jnp.float32), 0.25, 1.75).astype(jnp.bfloat16)
    w_query = scatter_about(arg_keys[4], (LAYERS, D, HQ * HD), D ** -0.5, 0.0625, ((0, 2), (1, 4), (2, 4)))
    w_key = scatter_about(arg_keys[5], (LAYERS, D, KVH * HD), D ** -0.5, 0.0625, ((0, 2), (1, 4), (2, 4)))
    w_value = scatter_about(arg_keys[6], (LAYERS, D, KVH * HD), D ** -0.5, 0.0625, ((0, 2), (1, 4), (2, 4)))
    w_out = scatter_about(arg_keys[7], (LAYERS, HQ * HD, D), (HQ * HD) ** -0.5, 0.0625, ((0, 2), (1, 4), (2, 4)))
    ffn_gain = jnp.clip(1.0 + 0.15 * jax.random.normal(arg_keys[8], (LAYERS, D), jnp.float32), 0.25, 1.75).astype(jnp.bfloat16)
    w_gate = scatter_about(arg_keys[9], (LAYERS, D, FF), D ** -0.5, 0.0625, ((0, 2), (1, 4), (2, 4)))
    w_up = scatter_about(arg_keys[10], (LAYERS, D, FF), D ** -0.5, 0.0625, ((0, 2), (1, 4), (2, 4)))
    w_down = scatter_about(arg_keys[11], (LAYERS, FF, D), FF ** -0.5, 0.046875, ((0, 2), (1, 4), (2, 4)))
    key_cache = draw_key_cache(jax.random.fold_in(arg_keys[14], 71), 0)
    value_cache = draw_value_cache(jax.random.fold_in(arg_keys[14], 71), 0)
    return dict(hidden_in=hidden_in, lengths=lengths, owner_order=owner_order, attn_gain=attn_gain, w_query=w_query, w_key=w_key, w_value=w_value, w_out=w_out, ffn_gain=ffn_gain, w_gate=w_gate, w_up=w_up, w_down=w_down, key_cache=key_cache, value_cache=value_cache)


epsilon = 1e-05
rope_base = 500000.0

def rotate(vectors, positions):
    size = vectors.shape[-1]
    half = size // 2
    freqs = rope_base ** (-(jnp.arange(half, dtype=jnp.float32) * 2.0) / size)
    angles = positions[:, None, None] * freqs[None, None, :]
    cosine = jnp.concatenate([jnp.cos(angles), jnp.cos(angles)], axis=-1)
    sine = jnp.concatenate([jnp.sin(angles), jnp.sin(angles)], axis=-1)
    turned = jnp.concatenate([-vectors[..., half:], vectors[..., :half]], axis=-1)
    return vectors * cosine + turned * sine

def scale_rows(states, norm_gain):
    as_float = states.astype(jnp.float32)
    factor = lax.rsqrt(lax.optimization_barrier(jnp.sum(as_float * as_float, axis=1)) / as_float.shape[1] + epsilon)
    scaled = (as_float * norm_gain.astype(jnp.float32)[None, :]).astype(jnp.bfloat16)
    return (scaled, factor)

def attend_one(request_item):
    queries, new_key, new_value, key_rows, value_rows, length = request_item
    kv_heads = new_key.shape[0]
    context = key_rows.shape[0]
    keys_float = key_rows.reshape(context, kv_heads, HD).astype(jnp.float32)
    values_float = value_rows.reshape(context, kv_heads, HD).astype(jnp.float32)
    queries_float = queries.astype(jnp.float32)
    score_scale = 1.0 / math.sqrt(HD)
    scores = jnp.einsum('grd,jgd->grj', queries_float, keys_float) * score_scale
    live_slots = jnp.arange(context, dtype=jnp.int32) < length
    scores = jnp.where(live_slots[None, None, :], scores, -jnp.inf)
    own_score = jnp.einsum('grd,gd->gr', queries_float, new_key.astype(jnp.float32)) * score_scale
    peak_score = jnp.maximum(lax.optimization_barrier(jnp.max(scores, axis=-1)), own_score)
    soft_weights = jnp.exp(scores - peak_score[..., None])
    own_weight = jnp.exp(own_score - peak_score)
    softmax_total = lax.optimization_barrier(jnp.sum(soft_weights, axis=-1)) + own_weight
    soft_rounded = lax.optimization_barrier(soft_weights.astype(jnp.bfloat16)).astype(jnp.float32)
    own_rounded = lax.optimization_barrier(own_weight.astype(jnp.bfloat16)).astype(jnp.float32)
    mixed_heads = jnp.einsum('grj,jgd->grd', soft_rounded, values_float)
    mixed_heads = mixed_heads + own_rounded[..., None] * new_value.astype(jnp.float32)[:, None, :]
    return (mixed_heads / softmax_total[..., None]).astype(jnp.bfloat16)

def decoder_layer(states, lengths, owner_order, attn_gain, w_query, w_key, w_value, w_out, ffn_gain, w_gate, w_up, w_down, key_rows, value_rows):
    request_count = states.shape[0]
    kv_heads = w_key.shape[1] // HD
    group_size = w_query.shape[1] // w_key.shape[1]
    scaled, factor = scale_rows(states, attn_gain)
    queries = (jnp.dot(scaled, w_query, preferred_element_type=jnp.float32) * factor[:, None]).reshape(request_count, -1, HD)
    new_keys = (jnp.dot(scaled, w_key, preferred_element_type=jnp.float32) * factor[:, None]).reshape(request_count, kv_heads, HD)
    new_values = (jnp.dot(scaled, w_value, preferred_element_type=jnp.float32) * factor[:, None]).reshape(request_count, kv_heads, HD)
    positions = lengths.astype(jnp.float32)
    queries = rotate(queries, positions).astype(jnp.bfloat16)
    new_keys = rotate(new_keys, positions).astype(jnp.bfloat16)
    new_values = new_values.astype(jnp.bfloat16)
    slot_queries = jnp.take(queries, owner_order, axis=0).reshape(request_count, kv_heads, group_size, HD)
    slot_keys = jnp.take(new_keys, owner_order, axis=0)
    slot_values = jnp.take(new_values, owner_order, axis=0)
    slot_lengths = jnp.take(lengths, owner_order, axis=0)
    attended = lax.map(attend_one, (slot_queries, slot_keys, slot_values, key_rows, value_rows, slot_lengths))
    attended = attended.reshape(request_count, -1)
    request_rows = jnp.zeros_like(attended).at[owner_order].set(attended)
    attention_out = jnp.dot(request_rows, w_out, preferred_element_type=jnp.float32)
    after_attention = (states.astype(jnp.float32) + attention_out).astype(jnp.bfloat16)
    scaled_second, factor_second = scale_rows(after_attention, ffn_gain)
    gate_sums = jnp.dot(scaled_second, w_gate, preferred_element_type=jnp.float32) * factor_second[:, None]
    up_sums = jnp.dot(scaled_second, w_up, preferred_element_type=jnp.float32) * factor_second[:, None]
    hidden = (jax.nn.silu(gate_sums) * up_sums).astype(jnp.bfloat16)
    down_terms = jnp.dot(hidden, w_down, preferred_element_type=jnp.float32)
    return (after_attention.astype(jnp.float32) + down_terms).astype(jnp.bfloat16)

def reference(hidden_in, lengths, owner_order, attn_gain, w_query, w_key, w_value, w_out, ffn_gain, w_gate, w_up, w_down, key_cache, value_cache):
    states = hidden_in
    results = []
    for layer_index in range(LAYERS):
        states = decoder_layer(states, lengths, owner_order, attn_gain[layer_index], w_query[layer_index], w_key[layer_index], w_value[layer_index], w_out[layer_index], ffn_gain[layer_index], w_gate[layer_index], w_up[layer_index], w_down[layer_index], key_cache[layer_index], value_cache[layer_index])
        results.append(states)
    return jnp.stack(results)
```

```python
import functools
import math

import jax
import jax.numpy as jnp
from jax import lax
from jax.experimental import pallas as pl
from jax.experimental.pallas import tpu as pltpu
from jax.sharding import PartitionSpec as P

HD = 128
EPSILON = 1e-05
ROPE_BASE = 500000.0
LANES = 128
F32 = jnp.float32
BF16 = jnp.bfloat16
IN_VMEM = pl.BlockSpec(memory_space=pltpu.VMEM)
IN_SMEM = pl.BlockSpec(memory_space=pltpu.SMEM)
MIB = 1 << 20


def run(kernel, outs, args, specs=None, scratch=(), grant=2, flops=0, name=None):
    single = isinstance(outs, tuple)
    out_list = [outs] if single else list(outs)
    moved = sum(a.size * a.dtype.itemsize for a in args)
    result = pl.pallas_call(
        kernel,
        out_shape=[jax.ShapeDtypeStruct(shape, dtype) for shape, dtype in out_list],
        in_specs=specs or [IN_VMEM] * len(args),
        out_specs=[IN_VMEM] * len(out_list),
        scratch_shapes=list(scratch),
        compiler_params=pltpu.CompilerParams(vmem_limit_bytes=grant * MIB),
        cost_estimate=pl.CostEstimate(flops=flops, bytes_accessed=moved, transcendentals=0),
        name=name,
    )(*args)
    return result[0] if single else result


def partners(values, axis):
    count = lax.axis_size(axis)
    return [
        lax.ppermute(values[s], axis, [(i, i ^ s) for i in range(count)]) for s in range(1, count)
    ]


def tree_sum(pieces):
    while len(pieces) > 1:
        pieces = [a + b for a, b in zip(pieces[::2], pieces[1::2])]
    return pieces[0]


def matmul_into(out_ref, start, rows, weight_ref, step):
    cols = weight_ref.shape[1]
    while cols % step:
        step //= 2

    def one(i, carry):
        at = pl.multiple_of(i * step, step)
        out_ref[:, pl.ds(start + at, step)] = jnp.dot(
            rows, weight_ref[:, pl.ds(at, step)], preferred_element_type=F32
        ).astype(out_ref.dtype)
        return carry

    lax.fori_loop(0, cols // step, one, 0)


def total_of(refs, rows=slice(None), cols=slice(None)):
    return tree_sum([ref[rows, cols].astype(F32) for ref in refs])


def heads_kernel(count, x_ref, gain_ref, perm_ref, wq_ref, wk_ref, wv_ref, *rest):
    out_refs, sums = rest[:count], rest[count]
    slots = x_ref.shape[0] // count
    x = jnp.dot(perm_ref[...], x_ref[...], preferred_element_type=F32)
    scaled = (x * gain_ref[...].astype(F32)).astype(BF16)
    squares = jnp.sum(x * x, axis=1, keepdims=True)
    at = 0
    for weight_ref in (wq_ref, wk_ref, wv_ref):
        matmul_into(sums, at, scaled, weight_ref, 512)
        at += weight_ref.shape[1]
    sums[:, at:] = jnp.broadcast_to(squares, (x.shape[0], LANES))
    for s in range(count):
        out_refs[s][...] = sums[s * slots : (s + 1) * slots, :]


def attention_kernel(count, width, kv_heads, lengths_ref, cos_ref, sin_ref, *rest):
    pieces = rest[:count]
    key_ref, value_ref, out_ref, head_scr, score_scr, row_scr = rest[count:]
    slots, context = key_ref.shape[:2]
    query_heads = out_ref.shape[1] // HD
    group = query_heads // kv_heads
    chunk = min(512, context)
    total = total_of(pieces)
    wide = total.shape[1]
    squares = total[:, wide - LANES : wide - LANES + 1]
    total = total[:, : wide - LANES] * lax.rsqrt(squares / width + EPSILON)
    all_heads = query_heads + 2 * kv_heads
    scale = 1.0 / math.sqrt(HD)
    lane = lax.broadcasted_iota(jnp.int32, (1, HD), 1)
    head_of = lax.broadcasted_iota(jnp.int32, (query_heads, 1), 0) // group
    for s in range(slots):
        for h in range(all_heads):
            head_scr[h : h + 1, :] = total[s : s + 1, h * HD : (h + 1) * HD]
        rotating = head_scr[: query_heads + kv_heads, :]
        rolled = pltpu.roll(rotating, HD // 2, 1)
        turned = jnp.where(lane < HD // 2, -rolled, rolled)
        rotated = (rotating * cos_ref[s : s + 1, :] + turned * sin_ref[s : s + 1, :]).astype(BF16)
        rotated = rotated.astype(F32)
        queries = rotated[:query_heads]
        new_key = jnp.zeros_like(queries)
        new_value = jnp.zeros_like(queries)
        spread = []
        for g in range(kv_heads):
            mine = head_of == g
            new_key = jnp.where(mine, rotated[query_heads + g : query_heads + g + 1], new_key)
            value_row = query_heads + kv_heads + g
            new_value = jnp.where(mine, head_scr[value_row : value_row + 1, :], new_value)
            spread.append(jnp.where(mine, queries, 0.0))
        spread = jnp.concatenate(spread, axis=1).astype(BF16)
        own_score = jnp.sum(queries * new_key, axis=1, keepdims=True) * scale
        new_value = new_value.astype(BF16).astype(F32)
        length = lengths_ref[s]
        chunks = (length + chunk - 1) // chunk

        def score(c, peak):
            at = pl.multiple_of(c * chunk, chunk)
            scores = lax.dot_general(
                spread,
                key_ref[s, pl.ds(at, chunk), :],
                (((1,), (1,)), ((), ())),
                preferred_element_type=F32,
            )
            position = at + lax.broadcasted_iota(jnp.int32, (1, chunk), 1)
            scores = jnp.where(position < length, scores * scale, -jnp.inf)
            score_scr[:, pl.ds(at, chunk)] = scores
            return jnp.maximum(peak, jnp.max(scores, axis=1, keepdims=True))

        peak = lax.fori_loop(0, chunks, score, own_score)
        own = jnp.exp(own_score - peak)

        def mix(c, carry):
            mixed, weight_sum = carry
            at = pl.multiple_of(c * chunk, chunk)
            soft = jnp.exp(score_scr[:, pl.ds(at, chunk)] - peak)
            mixed = mixed + jnp.dot(
                soft.astype(BF16), value_ref[s, pl.ds(at, chunk), :], preferred_element_type=F32
            )
            return mixed, weight_sum + jnp.sum(soft, axis=1, keepdims=True)

        mixed, weight_sum = lax.fori_loop(
            0,
            chunks,
            mix,
            (jnp.zeros((query_heads, kv_heads * HD), F32), jnp.zeros((query_heads, 1), F32)),
        )
        picked = jnp.zeros((query_heads, HD), F32)
        for g in range(kv_heads):
            picked = jnp.where(head_of == g, mixed[:, g * HD : (g + 1) * HD], picked)
        picked = picked + own.astype(BF16).astype(F32) * new_value
        head_scr[:query_heads, :] = picked / (weight_sum + own)
        for h in range(query_heads):
            row_scr[s : s + 1, h * HD : (h + 1) * HD] = head_scr[h : h + 1, :]
    out_ref[...] = row_scr[...].astype(BF16)


def project_kernel(count, perm_ref, w_ref, *rest):
    pieces = rest[:count]
    out_ref, rows_scr = rest[count:]
    slots = pieces[0].shape[0]
    for s in range(count):
        rows_scr[s * slots : (s + 1) * slots, :] = pieces[s][...].astype(F32)
    rows = jnp.dot(
        perm_ref[...], rows_scr[...].astype(BF16), preferred_element_type=F32
    ).astype(BF16)
    matmul_into(out_ref, 0, rows, w_ref, 512)


def hidden_terms_kernel(count, x_ref, gain_ref, wg_ref, wu_ref, *rest):
    pieces = rest[:count]
    after_ref, out_ref = rest[count:]
    after = (x_ref[...].astype(F32) + total_of(pieces)).astype(BF16)
    after_ref[...] = after
    after = after.astype(F32)
    scaled = (after * gain_ref[...].astype(F32)).astype(BF16)
    squares = jnp.broadcast_to(
        jnp.sum(after * after, axis=1, keepdims=True), (after.shape[0], LANES)
    )
    matmul_into(out_ref, 0, scaled, wg_ref, 512)
    matmul_into(out_ref, wg_ref.shape[1], scaled, wu_ref, 512)
    at = wg_ref.shape[1] + wu_ref.shape[1]
    for _ in range(3):
        part = squares.astype(BF16)
        out_ref[:, at : at + LANES] = part
        squares = squares - part.astype(F32)
        at += LANES


def down_kernel(count, width, w_ref, *rest):
    pieces = rest[:count]
    out_ref, hidden_scr = rest[count:]
    units = w_ref.shape[0]
    squares = tree_sum(
        [
            (
                ref[:, 2 * units : 2 * units + LANES].astype(F32)
                + ref[:, 2 * units + LANES : 2 * units + 2 * LANES].astype(F32)
            )
            + ref[:, 2 * units + 2 * LANES :].astype(F32)
            for ref in pieces
        ]
    )
    factor = lax.rsqrt(squares[:, :1] / width + EPSILON)
    step = 512
    while units % step:
        step //= 2
    for at in range(0, units, step):
        gate = total_of(pieces, cols=slice(at, at + step)) * factor
        up = total_of(pieces, cols=slice(units + at, units + at + step)) * factor
        hidden_scr[:, at : at + step] = (gate / (1.0 + jnp.exp(-gate)) * up).astype(BF16)
    matmul_into(out_ref, 0, hidden_scr[...], w_ref, 256)


def finish_kernel(count, x_ref, *rest):
    pieces = rest[:count]
    out_ref = rest[count]
    out_ref[...] = (x_ref[...].astype(F32) + total_of(pieces)).astype(BF16)


def choose_kernel(count, section_ref, x_ref, first_ref, *rest):
    pieces = rest[:count]
    out_ref = rest[count]
    second = (x_ref[...].astype(F32) + total_of(pieces)).astype(BF16).astype(F32)
    first = first_ref[...].astype(F32)
    out_ref[...] = jnp.where(section_ref[0] == 0, first, second).astype(BF16)


def per_device(
    hidden_in,
    lengths,
    owner_order,
    attn_gain,
    w_query,
    w_key,
    w_value,
    w_out,
    ffn_gain,
    w_gate,
    w_up,
    w_down,
    key_cache,
    value_cache,
):
    mems, tps = lax.axis_size("mem"), lax.axis_size("tp")
    requests, local_width = hidden_in.shape
    slots = requests // mems
    width = local_width * mems
    query_cols, kv_cols, units = w_query.shape[2], w_key.shape[2], w_gate.shape[2]
    kv_heads = kv_cols // HD
    me = lax.axis_index("mem")
    section = lax.axis_index("section").astype(jnp.int32).reshape(1)

    group = jnp.arange(requests, dtype=jnp.int32) // slots
    slot_index = (group ^ me) * slots + jnp.arange(requests, dtype=jnp.int32) % slots
    every = jnp.arange(requests, dtype=jnp.int32)
    request_of = jnp.sum(
        jnp.where(slot_index[:, None] == every[None, :], owner_order[None, :], 0), axis=1
    )
    here = request_of[:, None] == every[None, :]
    perm = here.astype(BF16)
    perm_back = (request_of[None, :] == every[:, None]).astype(BF16)
    slot_lengths = jnp.sum(jnp.where(here[:slots], lengths[None, :], 0), axis=1)
    freqs = ROPE_BASE ** (-(jnp.arange(HD // 2, dtype=F32) * 2.0) / HD)
    angles = slot_lengths.astype(F32)[:, None] * freqs[None, :]
    cosine = jnp.concatenate([jnp.cos(angles)] * 2, axis=-1)
    sine = jnp.concatenate([jnp.sin(angles)] * 2, axis=-1)

    head_cols = query_cols + 2 * kv_cols
    term_cols = 2 * units + 3 * LANES

    def layer(x, tag):
        heads = run(
            functools.partial(heads_kernel, mems),
            [((slots, head_cols + LANES), F32)] * mems,
            [x, attn_gain, perm, w_query[0], w_key[0], w_value[0]],
            scratch=[pltpu.VMEM((requests, head_cols + LANES), F32)],
            name="heads" + tag,
        )
        attended = run(
            functools.partial(attention_kernel, mems, width, kv_heads),
            ((slots, query_cols), BF16),
            [slot_lengths, cosine, sine, heads[0], *partners(heads, "mem"), key_cache[0], value_cache[0]],
            specs=[IN_SMEM] + [IN_VMEM] * (mems + 4),
            scratch=[
                pltpu.VMEM((-(-head_cols // HD // 8) * 8, HD), F32),
                pltpu.VMEM((query_cols // HD, key_cache.shape[2]), F32),
                pltpu.VMEM((slots, query_cols), F32),
            ],
            name="attention" + tag,
        )
        projected = run(
            functools.partial(project_kernel, mems),
            ((requests, local_width), BF16),
            [perm_back, w_out[0], attended, *partners([attended] * mems, "mem")],
            scratch=[pltpu.VMEM((requests, query_cols), F32)],
            name="project" + tag,
        )
        after, terms = run(
            functools.partial(hidden_terms_kernel, tps),
            [((requests, local_width), BF16), ((requests, term_cols), BF16)],
            [x, ffn_gain, w_gate[0], w_up[0], projected, *partners([projected] * tps, "tp")],
            name="terms" + tag,
        )
        down = run(
            functools.partial(down_kernel, mems, width),
            ((requests, local_width), BF16),
            [w_down[0], terms, *partners([terms] * mems, "mem")],
            scratch=[pltpu.VMEM((requests, units), BF16)],
            name="down" + tag,
        )
        return after, [down, *partners([down] * tps, "tp")]

    after, downs = layer(hidden_in, "_0")
    first = run(
        functools.partial(finish_kernel, tps),
        ((requests, local_width), BF16),
        [after, *downs],
        name="finish",
    )
    sections = lax.axis_size("section")
    passed = lax.ppermute(first, "section", [(i, (i + 1) % sections) for i in range(sections)])
    after, downs = layer(passed, "_1")
    result = run(
        functools.partial(choose_kernel, tps),
        ((requests, local_width), BF16),
        [section, after, first, *downs],
        specs=[IN_SMEM] + [IN_VMEM] * (tps + 2),
        name="choose",
    )
    return result[None]


def solution(mesh):
    placed = (
        P(None, "mem"),
        P(),
        P(),
        P("section", "mem"),
        P("section", "mem", "tp"),
        P("section", "mem", "tp"),
        P("section", "mem", "tp"),
        P("section", "tp", "mem"),
        P("section", "mem"),
        P("section", "mem", "tp"),
        P("section", "mem", "tp"),
        P("section", "tp", "mem"),
        P("section", "mem", None, "tp"),
        P("section", "mem", None, "tp"),
    )
    return jax.shard_map(
        per_device, mesh=mesh, in_specs=placed, out_specs=P("section", None, "mem"), check_vma=False
    )
```

```python
import functools
import math

import jax
import jax.numpy as jnp
from jax import lax
from jax.experimental import pallas as pl
from jax.experimental.pallas import tpu as pltpu
from jax.sharding import PartitionSpec as P

HD = 128
EPSILON = 1e-05
ROPE_BASE = 500000.0
LANES = 128
F32 = jnp.float32
BF16 = jnp.bfloat16
IN_VMEM = pl.BlockSpec(memory_space=pltpu.VMEM)
MIB = 1 << 20


STAGE_US = dict.fromkeys(("heads", "attention", "project", "terms", "down", "window"), 20)


def run(kernel, outs, args, specs=None, scratch=(), grant=2, name=None, keep=()):
    single = isinstance(outs, tuple)
    out_list = [outs] if single else list(outs)
    flops = STAGE_US.get(name.split("_")[0], 0) * 1150000000
    args, held = list(args), len(args)

    def without_kept(*refs):
        kernel(*refs[:held], *refs[held + len(keep) :])

    result = pl.pallas_call(
        without_kept,
        out_shape=[jax.ShapeDtypeStruct(shape, dtype) for shape, dtype in out_list],
        in_specs=(specs or [IN_VMEM] * held) + [IN_VMEM] * len(keep),
        out_specs=[IN_VMEM] * len(out_list),
        scratch_shapes=list(scratch),
        compiler_params=pltpu.CompilerParams(vmem_limit_bytes=grant * MIB),
        cost_estimate=pl.CostEstimate(flops=flops, bytes_accessed=0, transcendentals=0),
        name=name,
    )(*args, *keep)
    return result[0] if single else result


def partners(values, axis):
    count = lax.axis_size(axis)
    return [
        lax.ppermute(values[s], axis, [(i, i ^ s) for i in range(count)]) for s in range(1, count)
    ]


def tree_sum(pieces):
    while len(pieces) > 1:
        pieces = [a + b for a, b in zip(pieces[::2], pieces[1::2])]
    return pieces[0]


def matmul_into(out_ref, start, rows, weight_ref, step):
    cols = weight_ref.shape[1]
    for at in range(0, cols, step):
        end = min(at + step, cols)
        out_ref[:, start + at : start + end] = jnp.dot(
            rows, weight_ref[:, at:end], preferred_element_type=F32
        ).astype(out_ref.dtype)


def total_of(refs, rows=slice(None), cols=slice(None)):
    return tree_sum([ref[rows, cols].astype(F32) for ref in refs])


def heads_kernel(count, x_ref, gain_ref, perm_ref, wq_ref, wk_ref, wv_ref, *rest):
    out_refs, sums = rest[:count], rest[count]
    slots = x_ref.shape[0] // count
    x = jnp.dot(perm_ref[...], x_ref[...], preferred_element_type=F32)
    scaled = (x * gain_ref[...].astype(F32)).astype(BF16)
    squares = jnp.sum(x * x, axis=1, keepdims=True)
    at = 0
    for weight_ref in (wq_ref, wk_ref, wv_ref):
        matmul_into(sums, at, scaled, weight_ref, 512)
        at += weight_ref.shape[1]
    sums[:, at:] = jnp.broadcast_to(squares, (x.shape[0], LANES))
    for s in range(count):
        out_refs[s][...] = sums[s * slots : (s + 1) * slots, :]


def first_heads_kernel(count, pieces, x_any, gain_any, owner_any, wq_any, wk_any, wv_any, *rest):
    out_refs = rest[:count]
    x_ref, gain_ref, owner, wq_ref, wk_ref, wv_ref, sums, sems = rest[count:]
    depth, query_cols = wq_ref.shape
    kv_cols = wk_ref.shape[1]
    rows = depth // pieces
    small = [
        pltpu.make_async_copy(source, target, sems.at[i])
        for i, (source, target) in enumerate(
            ((x_any, x_ref), (gain_any, gain_ref), (owner_any, owner), (wk_any, wk_ref), (wv_any, wv_ref))
        )
    ]
    large = [
        pltpu.make_async_copy(
            wq_any.at[p * rows : (p + 1) * rows], wq_ref.at[p * rows : (p + 1) * rows], sems.at[5 + p]
        )
        for p in range(pieces)
    ]
    for copy in small[:3] + large + small[3:]:
        copy.start()
    for copy in small[:3]:
        copy.wait()
    x = x_ref[...].astype(F32)
    scaled = (x * gain_ref[...].astype(F32)).astype(BF16)
    squares = jnp.sum(x * x, axis=1, keepdims=True)
    end = query_cols + 2 * kv_cols
    sums[:, end:] = jnp.broadcast_to(squares, (x.shape[0], LANES))
    for p in range(pieces):
        large[p].wait()
        part = jnp.dot(
            scaled[:, p * rows : (p + 1) * rows],
            wq_ref[p * rows : (p + 1) * rows, :],
            preferred_element_type=F32,
        )
        sums[:, :query_cols] = part if p == 0 else sums[:, :query_cols] + part
    for copy, weight_ref, at in ((small[3], wk_ref, query_cols), (small[4], wv_ref, query_cols + kv_cols)):
        copy.wait()
        matmul_into(sums, at, scaled, weight_ref, 512)
    slots = x.shape[0] // count
    me = lax.axis_index("mem")
    for s in range(count):
        for k in range(slots):
            request = owner[(me ^ s) * slots + k]
            out_refs[s][k : k + 1, :] = sums[pl.ds(request, 1), :]


def attention_kernel(count, width, kv_heads, lengths_ref, cos_ref, sin_ref, *rest):
    pieces = rest[:count]
    key_ref, value_ref = rest[count : count + 2]
    out_ref, head_scr, score_scr, row_scr = rest[count + 2 :]
    slots, context = key_ref.shape[:2]
    query_heads = out_ref.shape[1] // HD
    group = query_heads // kv_heads
    chunk = min(1024, context)
    total = total_of(pieces)
    wide = total.shape[1]
    squares = total[:, wide - LANES : wide - LANES + 1]
    total = total[:, : wide - LANES] * lax.rsqrt(squares / width + EPSILON)
    all_heads = query_heads + 2 * kv_heads
    scale = 1.0 / math.sqrt(HD)
    lane = lax.broadcasted_iota(jnp.int32, (1, HD), 1)
    head_of = lax.broadcasted_iota(jnp.int32, (query_heads, 1), 0) // group
    for s in range(slots):
        for h in range(all_heads):
            head_scr[s, h : h + 1, :] = total[s : s + 1, h * HD : (h + 1) * HD]
    spreads, own_scores, new_values, peaks = [], [], [], []
    for s in range(slots):
        rotating = head_scr[s, : query_heads + kv_heads, :]
        rolled = pltpu.roll(rotating, HD // 2, 1)
        turned = jnp.where(lane < HD // 2, -rolled, rolled)
        rotated = (rotating * cos_ref[s : s + 1, :] + turned * sin_ref[s : s + 1, :]).astype(BF16)
        rotated = rotated.astype(F32)
        queries = rotated[:query_heads]
        new_key = jnp.zeros_like(queries)
        new_value = jnp.zeros_like(queries)
        spread = []
        for g in range(kv_heads):
            mine = head_of == g
            new_key = jnp.where(mine, rotated[query_heads + g : query_heads + g + 1], new_key)
            value_row = query_heads + kv_heads + g
            new_value = jnp.where(mine, head_scr[s, value_row : value_row + 1, :], new_value)
            spread.append(jnp.where(mine, queries, 0.0))
        spreads.append(jnp.concatenate(spread, axis=1).astype(BF16))
        own_scores.append(jnp.sum(queries * new_key, axis=1, keepdims=True) * scale)
        new_values.append(new_value.astype(BF16).astype(F32))
        peaks.append(jnp.full((query_heads, LANES), -jnp.inf, F32))
    position = lax.broadcasted_iota(jnp.int32, (1, chunk), 1)
    for at in range(0, context, chunk):
        for s in range(slots):
            scores = lax.dot_general(
                spreads[s],
                key_ref[s, at : at + chunk, :],
                (((1,), (1,)), ((), ())),
                preferred_element_type=F32,
            )
            scores = jnp.where(position + at < lengths_ref[s : s + 1, :1], scores * scale, -jnp.inf)
            score_scr[s, :, at : at + chunk] = scores
            for i in range(0, chunk, LANES):
                peaks[s] = jnp.maximum(peaks[s], scores[:, i : i + LANES])
    owns, sums, mixes = [], [], []
    for s in range(slots):
        peaks[s] = jnp.maximum(jnp.max(peaks[s], axis=1, keepdims=True), own_scores[s])
        owns.append(jnp.exp(own_scores[s] - peaks[s]))
        sums.append(jnp.zeros((query_heads, LANES), F32))
        mixes.append(jnp.zeros((query_heads, kv_heads * HD), F32))
    for at in range(0, context, chunk):
        for s in range(slots):
            soft = jnp.exp(score_scr[s, :, at : at + chunk] - peaks[s])
            for i in range(0, chunk, LANES):
                sums[s] = sums[s] + soft[:, i : i + LANES]
            mixes[s] = mixes[s] + jnp.dot(
                soft.astype(BF16), value_ref[s, at : at + chunk, :], preferred_element_type=F32
            )
    for s in range(slots):
        picked = jnp.zeros((query_heads, HD), F32)
        for g in range(kv_heads):
            picked = jnp.where(head_of == g, mixes[s][:, g * HD : (g + 1) * HD], picked)
        picked = picked + owns[s].astype(BF16).astype(F32) * new_values[s]
        total_weight = jnp.sum(sums[s], axis=1, keepdims=True) + owns[s]
        head_scr[s, :query_heads, :] = picked / total_weight
    for s in range(slots):
        for h in range(query_heads):
            row_scr[s : s + 1, h * HD : (h + 1) * HD] = head_scr[s, h : h + 1, :]
    out_ref[...] = row_scr[...].astype(BF16)


def project_kernel(count, perm_ref, w_ref, *rest):
    pieces = rest[:count]
    out_ref, rows_scr = rest[count:]
    slots = pieces[0].shape[0]
    for s in range(count):
        rows_scr[s * slots : (s + 1) * slots, :] = pieces[s][...].astype(F32)
    rows = jnp.dot(
        perm_ref[...], rows_scr[...].astype(BF16), preferred_element_type=F32
    ).astype(BF16)
    matmul_into(out_ref, 0, rows, w_ref, 512)


def hidden_terms_kernel(count, x_ref, gain_ref, wg_ref, wu_ref, *rest):
    pieces = rest[:count]
    after_ref, out_ref = rest[count:]
    after = (x_ref[...].astype(F32) + total_of(pieces)).astype(BF16)
    after_ref[...] = after
    after = after.astype(F32)
    scaled = (after * gain_ref[...].astype(F32)).astype(BF16)
    squares = jnp.broadcast_to(
        jnp.sum(after * after, axis=1, keepdims=True), (after.shape[0], LANES)
    )
    matmul_into(out_ref, 0, scaled, wg_ref, 512)
    matmul_into(out_ref, wg_ref.shape[1], scaled, wu_ref, 512)
    at = wg_ref.shape[1] + wu_ref.shape[1]
    for _ in range(3):
        part = squares.astype(BF16)
        out_ref[:, at : at + LANES] = part
        squares = squares - part.astype(F32)
        at += LANES


def down_kernel(count, width, w_ref, *rest):
    pieces = rest[:count]
    out_ref, hidden_scr = rest[count:]
    units = w_ref.shape[0]
    squares = tree_sum(
        [
            (
                ref[:, 2 * units : 2 * units + LANES].astype(F32)
                + ref[:, 2 * units + LANES : 2 * units + 2 * LANES].astype(F32)
            )
            + ref[:, 2 * units + 2 * LANES :].astype(F32)
            for ref in pieces
        ]
    )
    factor = lax.rsqrt(squares[:, :1] / width + EPSILON)
    step = 512
    while units % step:
        step //= 2
    for at in range(0, units, step):
        gate = total_of(pieces, cols=slice(at, at + step)) * factor
        up = total_of(pieces, cols=slice(units + at, units + at + step)) * factor
        hidden_scr[:, at : at + step] = (gate / (1.0 + jnp.exp(-gate)) * up).astype(BF16)
    matmul_into(out_ref, 0, hidden_scr[...], w_ref, 512)


def finish_kernel(count, x_ref, *rest):
    pieces = rest[:count]
    out_ref = rest[count]
    out_ref[...] = (x_ref[...].astype(F32) + total_of(pieces)).astype(BF16)


def choose_kernel(count, x_ref, first_ref, *rest):
    pieces = rest[:count]
    out_ref = rest[count]
    second = (x_ref[...].astype(F32) + total_of(pieces)).astype(BF16).astype(F32)
    first = first_ref[...].astype(F32)
    out_ref[...] = jnp.where(lax.axis_index("section") == 0, first, second).astype(BF16)


def per_device(
    hidden_in,
    lengths,
    owner_order,
    attn_gain,
    w_query,
    w_key,
    w_value,
    w_out,
    ffn_gain,
    w_gate,
    w_up,
    w_down,
    key_cache,
    value_cache,
):
    mems, tps = lax.axis_size("mem"), lax.axis_size("tp")
    requests, local_width = hidden_in.shape
    slots = requests // mems
    width = local_width * mems
    query_cols, kv_cols, units = w_query.shape[2], w_key.shape[2], w_gate.shape[2]
    kv_heads = kv_cols // HD
    me = lax.axis_index("mem")

    group = jnp.arange(requests, dtype=jnp.int32) // slots
    slot_index = (group ^ me) * slots + jnp.arange(requests, dtype=jnp.int32) % slots
    every = jnp.arange(requests, dtype=jnp.int32)
    request_of = jnp.sum(
        jnp.where(slot_index[:, None] == every[None, :], owner_order[None, :], 0), axis=1
    )
    here = request_of[:, None] == every[None, :]
    perm = here.astype(BF16)
    perm_back = (request_of[None, :] == every[:, None]).astype(BF16)
    slot_lengths = jnp.sum(jnp.where(here[:slots], lengths[None, :], 0), axis=1)
    wide_lengths = jnp.broadcast_to(slot_lengths[:, None], (slots, LANES))
    freqs = ROPE_BASE ** (-(jnp.arange(HD // 2, dtype=F32) * 2.0) / HD)
    angles = slot_lengths.astype(F32)[:, None] * freqs[None, :]
    cosine = jnp.concatenate([jnp.cos(angles)] * 2, axis=-1)
    sine = jnp.concatenate([jnp.sin(angles)] * 2, axis=-1)

    head_cols = query_cols + 2 * kv_cols
    term_cols = 2 * units + 3 * LANES

    def first_heads():
        pieces = 8
        return run(
            functools.partial(first_heads_kernel, mems, pieces),
            [((slots, head_cols + LANES), F32)] * mems,
            [
                pltpu.with_memory_space_constraint(source, pltpu.HBM)
                for source in (hidden_in, attn_gain, owner_order, w_query[0], w_key[0], w_value[0])
            ],
            specs=[pl.BlockSpec(memory_space=pltpu.HBM)] * 6,
            scratch=[
                pltpu.VMEM((requests, local_width), BF16),
                pltpu.VMEM((1, local_width), BF16),
                pltpu.SMEM((requests,), jnp.int32),
                pltpu.VMEM((local_width, query_cols), BF16),
                pltpu.VMEM((local_width, kv_cols), BF16),
                pltpu.VMEM((local_width, kv_cols), BF16),
                pltpu.VMEM((requests, head_cols + LANES), F32),
                pltpu.SemaphoreType.DMA((5 + pieces,)),
            ],
            grant=12,
            name="heads_0",
        )

    def heads_of(x, tag):
        return run(
            functools.partial(heads_kernel, mems),
            [((slots, head_cols + LANES), F32)] * mems,
            [x, attn_gain, perm, w_query[0], w_key[0], w_value[0]],
            scratch=[pltpu.VMEM((requests, head_cols + LANES), F32)],
            name="heads" + tag,
        )

    def window(value, after):
        def kernel(value_ref, after_ref, out_ref):
            out_ref[...] = value_ref[...]

        return run(kernel, (value.shape, value.dtype), [value, after], name="window")

    def layer(x, heads, tag):
        attended = run(
            functools.partial(attention_kernel, mems, width, kv_heads),
            ((slots, query_cols), BF16),
            [
                wide_lengths,
                window(cosine, heads[0]) if tag == "_0" else cosine,
                sine,
                heads[0],
                *partners(heads, "mem"),
                key_cache[0],
                value_cache[0],
            ],
            scratch=[
                pltpu.VMEM((slots, -(-head_cols // HD // 8) * 8, HD), F32),
                pltpu.VMEM((slots, query_cols // HD, key_cache.shape[2]), F32),
                pltpu.VMEM((slots, query_cols), F32),
            ],
            grant=3,
            name="attention" + tag,
        )
        projected = run(
            functools.partial(project_kernel, mems),
            ((requests, local_width), BF16),
            [perm_back, w_out[0], attended, *partners([attended] * mems, "mem")],
            scratch=[pltpu.VMEM((requests, query_cols), F32)],
            name="project" + tag,
        )
        after, terms = run(
            functools.partial(hidden_terms_kernel, tps),
            [((requests, local_width), BF16), ((requests, term_cols), BF16)],
            [x, ffn_gain, w_gate[0], w_up[0], projected, *partners([projected] * tps, "tp")],
            name="terms" + tag,
        )
        down = run(
            functools.partial(down_kernel, mems, width),
            ((requests, local_width), BF16),
            [w_down[0], terms, *partners([terms] * mems, "mem")],
            scratch=[pltpu.VMEM((requests, units), BF16)],
            keep=[window(cosine, terms)] if tag == "_1" else (),
            name="down" + tag,
        )
        return after, [down, *partners([down] * tps, "tp")]

    after, downs = layer(hidden_in, first_heads(), "_0")
    first = run(
        functools.partial(finish_kernel, tps),
        ((requests, local_width), BF16),
        [after, *downs],
        name="finish",
    )
    sections = lax.axis_size("section")
    passed = lax.ppermute(first, "section", [(i, (i + 1) % sections) for i in range(sections)])
    after, downs = layer(passed, heads_of(passed, "_1"), "_1")
    result = run(
        functools.partial(choose_kernel, tps),
        ((requests, local_width), BF16),
        [after, first, *downs],
        name="choose",
    )
    return result[None]


def solution(mesh):
    placed = (
        P(None, "mem"),
        P(),
        P(),
        P("section", "mem"),
        P("section", "mem", "tp"),
        P("section", "mem", "tp"),
        P("section", "mem", "tp"),
        P("section", "tp", "mem"),
        P("section", "mem"),
        P("section", "mem", "tp"),
        P("section", "mem", "tp"),
        P("section", "tp", "mem"),
        P("section", "mem", None, "tp"),
        P("section", "mem", None, "tp"),
    )
    return jax.shard_map(
        per_device, mesh=mesh, in_specs=placed, out_specs=P("section", None, "mem"), check_vma=False
    )
```

```python
import functools
import math

import jax
import jax.numpy as jnp
from jax import lax
from jax.experimental import pallas as pl
from jax.experimental.pallas import tpu as pltpu
from jax.sharding import PartitionSpec as P

HD = 128
EPSILON = 1e-05
ROPE_BASE = 500000.0
LANES = 128
F32 = jnp.float32
BF16 = jnp.bfloat16
IN_VMEM = pl.BlockSpec(memory_space=pltpu.VMEM)
MIB = 1 << 20


STAGE_US = dict.fromkeys(("heads", "attention", "project", "terms", "down", "window"), 20)


def run(kernel, outs, args, specs=None, scratch=(), grant=2, name=None, keep=(), section=None):
    single = isinstance(outs, tuple)
    out_list = [outs] if single else list(outs)
    flops = STAGE_US.get(name.split("_")[0], 0) * 1150000000
    args, held = list(args), len(args)
    first_out = held + len(keep)

    def in_section(*refs):
        def work():
            kernel(*refs[:held], *refs[first_out:])

        if section is None:
            return work()
        here = lax.axis_index("section") == section
        pl.when(here)(work)

        @pl.when(jnp.logical_not(here))
        def _():
            for out_ref in refs[first_out : first_out + len(out_list)]:
                out_ref[...] = jnp.zeros_like(out_ref)

    result = pl.pallas_call(
        in_section,
        out_shape=[jax.ShapeDtypeStruct(shape, dtype) for shape, dtype in out_list],
        in_specs=(specs or [IN_VMEM] * held) + [IN_VMEM] * len(keep),
        out_specs=[IN_VMEM] * len(out_list),
        scratch_shapes=list(scratch),
        compiler_params=pltpu.CompilerParams(vmem_limit_bytes=grant * MIB),
        cost_estimate=pl.CostEstimate(flops=flops, bytes_accessed=0, transcendentals=0),
        name=name,
    )(*args, *keep)
    return result[0] if single else result


def partners(values, axis):
    count = lax.axis_size(axis)
    return [
        lax.ppermute(values[s], axis, [(i, i ^ s) for i in range(count)]) for s in range(1, count)
    ]


def tree_sum(pieces):
    while len(pieces) > 1:
        pieces = [a + b for a, b in zip(pieces[::2], pieces[1::2])]
    return pieces[0]


def matmul_into(out_ref, start, rows, weight_ref, step):
    cols = weight_ref.shape[1]
    for at in range(0, cols, step):
        end = min(at + step, cols)
        out_ref[:, start + at : start + end] = jnp.dot(
            rows, weight_ref[:, at:end], preferred_element_type=F32
        ).astype(out_ref.dtype)


def total_of(refs, rows=slice(None), cols=slice(None)):
    return tree_sum([ref[rows, cols].astype(F32) for ref in refs])


def heads_kernel(count, x_ref, gain_ref, perm_ref, wq_ref, wk_ref, wv_ref, *rest):
    out_refs, sums = rest[:count], rest[count]
    slots = x_ref.shape[0] // count
    x = jnp.dot(perm_ref[...], x_ref[...], preferred_element_type=F32)
    scaled = (x * gain_ref[...].astype(F32)).astype(BF16)
    squares = jnp.sum(x * x, axis=1, keepdims=True)
    at = 0
    for weight_ref in (wq_ref, wk_ref, wv_ref):
        matmul_into(sums, at, scaled, weight_ref, 512)
        at += weight_ref.shape[1]
    sums[:, at:] = jnp.broadcast_to(squares, (x.shape[0], LANES))
    for s in range(count):
        out_refs[s][...] = sums[s * slots : (s + 1) * slots, :]


def first_heads_kernel(count, pieces, x_any, gain_any, owner_any, wq_any, wk_any, wv_any, *rest):
    out_refs = rest[:count]
    x_ref, gain_ref, owner, wq_ref, wk_ref, wv_ref, sums, sems = rest[count:]
    depth, query_cols = wq_ref.shape
    kv_cols = wk_ref.shape[1]
    rows = depth // pieces
    small = [
        pltpu.make_async_copy(source, target, sems.at[i])
        for i, (source, target) in enumerate(
            ((x_any, x_ref), (gain_any, gain_ref), (owner_any, owner), (wk_any, wk_ref), (wv_any, wv_ref))
        )
    ]
    large = [
        pltpu.make_async_copy(
            wq_any.at[p * rows : (p + 1) * rows], wq_ref.at[p * rows : (p + 1) * rows], sems.at[5 + p]
        )
        for p in range(pieces)
    ]
    for copy in small[:3] + large + small[3:]:
        copy.start()
    for copy in small[:3]:
        copy.wait()
    x = x_ref[...].astype(F32)
    scaled = (x * gain_ref[...].astype(F32)).astype(BF16)
    squares = jnp.sum(x * x, axis=1, keepdims=True)
    end = query_cols + 2 * kv_cols
    sums[:, end:] = jnp.broadcast_to(squares, (x.shape[0], LANES))
    for p in range(pieces):
        large[p].wait()
        part = jnp.dot(
            scaled[:, p * rows : (p + 1) * rows],
            wq_ref[p * rows : (p + 1) * rows, :],
            preferred_element_type=F32,
        )
        sums[:, :query_cols] = part if p == 0 else sums[:, :query_cols] + part
    for copy, weight_ref, at in ((small[3], wk_ref, query_cols), (small[4], wv_ref, query_cols + kv_cols)):
        copy.wait()
        matmul_into(sums, at, scaled, weight_ref, 512)
    slots = x.shape[0] // count
    me = lax.axis_index("mem")
    for s in range(count):
        for k in range(slots):
            request = owner[(me ^ s) * slots + k]
            out_refs[s][k : k + 1, :] = sums[pl.ds(request, 1), :]


def attention_kernel(count, width, kv_heads, lengths_ref, cos_ref, sin_ref, *rest):
    pieces = [rest[0], *rest[count - 1 : 0 : -1]]
    key_ref, value_ref = rest[count : count + 2]
    out_ref, head_scr, score_scr, row_scr = rest[count + 2 :]
    slots, context = key_ref.shape[:2]
    query_heads = out_ref.shape[1] // HD
    group = query_heads // kv_heads
    chunk = min(1024, context)
    total = total_of(pieces)
    wide = total.shape[1]
    squares = total[:, wide - LANES : wide - LANES + 1]
    total = total[:, : wide - LANES] * lax.rsqrt(squares / width + EPSILON)
    all_heads = query_heads + 2 * kv_heads
    scale = 1.0 / math.sqrt(HD)
    lane = lax.broadcasted_iota(jnp.int32, (1, HD), 1)
    head_of = lax.broadcasted_iota(jnp.int32, (query_heads, 1), 0) // group
    for s in range(slots):
        for h in range(all_heads):
            head_scr[s, h : h + 1, :] = total[s : s + 1, h * HD : (h + 1) * HD]
    spreads, own_scores, new_values, peaks = [], [], [], []
    for s in range(slots):
        rotating = head_scr[s, : query_heads + kv_heads, :]
        rolled = pltpu.roll(rotating, HD // 2, 1)
        turned = jnp.where(lane < HD // 2, -rolled, rolled)
        rotated = (rotating * cos_ref[s : s + 1, :] + turned * sin_ref[s : s + 1, :]).astype(BF16)
        rotated = rotated.astype(F32)
        queries = rotated[:query_heads]
        new_key = jnp.zeros_like(queries)
        new_value = jnp.zeros_like(queries)
        spread = []
        for g in range(kv_heads):
            mine = head_of == g
            new_key = jnp.where(mine, rotated[query_heads + g : query_heads + g + 1], new_key)
            value_row = query_heads + kv_heads + g
            new_value = jnp.where(mine, head_scr[s, value_row : value_row + 1, :], new_value)
            spread.append(jnp.where(mine, queries, 0.0))
        spreads.append(jnp.concatenate(spread, axis=1).astype(BF16))
        own_scores.append(jnp.sum(queries * new_key, axis=1, keepdims=True) * scale)
        new_values.append(new_value.astype(BF16).astype(F32))
        peaks.append(jnp.full((query_heads, LANES), -jnp.inf, F32))
    position = lax.broadcasted_iota(jnp.int32, (1, chunk), 1)
    for at in range(0, context, chunk):
        for s in range(slots):
            scores = lax.dot_general(
                spreads[s],
                key_ref[s, at : at + chunk, :],
                (((1,), (1,)), ((), ())),
                preferred_element_type=F32,
            )
            scores = jnp.where(position + at < lengths_ref[s : s + 1, :1], scores * scale, -jnp.inf)
            score_scr[s, :, at : at + chunk] = scores
            for i in range(0, chunk, LANES):
                peaks[s] = jnp.maximum(peaks[s], scores[:, i : i + LANES])
    owns, sums, mixes = [], [], []
    for s in range(slots):
        peaks[s] = jnp.maximum(jnp.max(peaks[s], axis=1, keepdims=True), own_scores[s])
        owns.append(jnp.exp(own_scores[s] - peaks[s]))
        sums.append(jnp.zeros((query_heads, LANES), F32))
        mixes.append(jnp.zeros((query_heads, kv_heads * HD), F32))
    for at in range(0, context, chunk):
        for s in range(slots):
            soft = jnp.exp(score_scr[s, :, at : at + chunk] - peaks[s])
            for i in range(0, chunk, LANES):
                sums[s] = sums[s] + soft[:, i : i + LANES]
            mixes[s] = mixes[s] + jnp.dot(
                soft.astype(BF16), value_ref[s, at : at + chunk, :], preferred_element_type=F32
            )
    for s in range(slots):
        picked = jnp.zeros((query_heads, HD), F32)
        for g in range(kv_heads):
            picked = jnp.where(head_of == g, mixes[s][:, g * HD : (g + 1) * HD], picked)
        picked = picked + owns[s].astype(BF16).astype(F32) * new_values[s]
        total_weight = jnp.sum(sums[s], axis=1, keepdims=True) + owns[s]
        head_scr[s, :query_heads, :] = picked / total_weight
    for s in range(slots):
        for h in range(query_heads):
            row_scr[s : s + 1, h * HD : (h + 1) * HD] = head_scr[s, h : h + 1, :]
    out_ref[...] = row_scr[...].astype(BF16)


def project_kernel(count, perm_ref, w_ref, *rest):
    pieces = rest[:count]
    out_ref, rows_scr = rest[count:]
    slots = pieces[0].shape[0]
    for s in range(count):
        rows_scr[s * slots : (s + 1) * slots, :] = pieces[s][...].astype(F32)
    rows = jnp.dot(
        perm_ref[...], rows_scr[...].astype(BF16), preferred_element_type=F32
    ).astype(BF16)
    matmul_into(out_ref, 0, rows, w_ref, 512)


def hidden_terms_kernel(count, x_ref, gain_ref, wg_ref, wu_ref, *rest):
    pieces = rest[:count]
    after_ref, out_ref = rest[count:]
    after = (x_ref[...].astype(F32) + total_of(pieces)).astype(BF16)
    after_ref[...] = after
    after = after.astype(F32)
    scaled = (after * gain_ref[...].astype(F32)).astype(BF16)
    squares = jnp.broadcast_to(
        jnp.sum(after * after, axis=1, keepdims=True), (after.shape[0], LANES)
    )
    matmul_into(out_ref, 0, scaled, wg_ref, 512)
    matmul_into(out_ref, wg_ref.shape[1], scaled, wu_ref, 512)
    at = wg_ref.shape[1] + wu_ref.shape[1]
    for _ in range(3):
        part = squares.astype(BF16)
        out_ref[:, at : at + LANES] = part
        squares = squares - part.astype(F32)
        at += LANES


def down_kernel(count, width, w_ref, *rest):
    pieces = rest[:count]
    out_ref, hidden_scr = rest[count:]
    units = w_ref.shape[0]
    squares = tree_sum(
        [
            (
                ref[:, 2 * units : 2 * units + LANES].astype(F32)
                + ref[:, 2 * units + LANES : 2 * units + 2 * LANES].astype(F32)
            )
            + ref[:, 2 * units + 2 * LANES :].astype(F32)
            for ref in pieces
        ]
    )
    factor = lax.rsqrt(squares[:, :1] / width + EPSILON)
    step = 512
    while units % step:
        step //= 2
    for at in range(0, units, step):
        gate = total_of(pieces, cols=slice(at, at + step)) * factor
        up = total_of(pieces, cols=slice(units + at, units + at + step)) * factor
        hidden_scr[:, at : at + step] = (gate / (1.0 + jnp.exp(-gate)) * up).astype(BF16)
    matmul_into(out_ref, 0, hidden_scr[...], w_ref, 512)


def finish_kernel(count, x_ref, *rest):
    pieces = rest[:count]
    out_ref = rest[count]
    out_ref[...] = (x_ref[...].astype(F32) + total_of(pieces)).astype(BF16)


def choose_kernel(count, x_ref, first_ref, *rest):
    pieces = rest[:count]
    out_ref = rest[count]
    second = (x_ref[...].astype(F32) + total_of(pieces)).astype(BF16).astype(F32)
    first = first_ref[...].astype(F32)
    out_ref[...] = jnp.where(lax.axis_index("section") == 0, first, second).astype(BF16)


def per_device(
    hidden_in,
    lengths,
    owner_order,
    attn_gain,
    w_query,
    w_key,
    w_value,
    w_out,
    ffn_gain,
    w_gate,
    w_up,
    w_down,
    key_cache,
    value_cache,
):
    mems, tps = lax.axis_size("mem"), lax.axis_size("tp")
    requests, local_width = hidden_in.shape
    slots = requests // mems
    width = local_width * mems
    query_cols, kv_cols, units = w_query.shape[2], w_key.shape[2], w_gate.shape[2]
    kv_heads = kv_cols // HD
    me = lax.axis_index("mem")

    group = jnp.arange(requests, dtype=jnp.int32) // slots
    slot_index = (group ^ me) * slots + jnp.arange(requests, dtype=jnp.int32) % slots
    every = jnp.arange(requests, dtype=jnp.int32)
    request_of = jnp.sum(
        jnp.where(slot_index[:, None] == every[None, :], owner_order[None, :], 0), axis=1
    )
    here = request_of[:, None] == every[None, :]
    perm = here.astype(BF16)
    perm_back = (request_of[None, :] == every[:, None]).astype(BF16)
    slot_lengths = jnp.sum(jnp.where(here[:slots], lengths[None, :], 0), axis=1)
    wide_lengths = jnp.broadcast_to(slot_lengths[:, None], (slots, LANES))
    freqs = ROPE_BASE ** (-(jnp.arange(HD // 2, dtype=F32) * 2.0) / HD)
    angles = slot_lengths.astype(F32)[:, None] * freqs[None, :]
    cosine = jnp.concatenate([jnp.cos(angles)] * 2, axis=-1)
    sine = jnp.concatenate([jnp.sin(angles)] * 2, axis=-1)

    head_cols = query_cols + 2 * kv_cols
    term_cols = 2 * units + 3 * LANES

    def first_heads():
        pieces = 8
        return run(
            functools.partial(first_heads_kernel, mems, pieces),
            [((slots, head_cols + LANES), F32)] * mems,
            [
                pltpu.with_memory_space_constraint(source, pltpu.HBM)
                for source in (hidden_in, attn_gain, owner_order, w_query[0], w_key[0], w_value[0])
            ],
            specs=[pl.BlockSpec(memory_space=pltpu.HBM)] * 6,
            scratch=[
                pltpu.VMEM((requests, local_width), BF16),
                pltpu.VMEM((1, local_width), BF16),
                pltpu.SMEM((requests,), jnp.int32),
                pltpu.VMEM((local_width, query_cols), BF16),
                pltpu.VMEM((local_width, kv_cols), BF16),
                pltpu.VMEM((local_width, kv_cols), BF16),
                pltpu.VMEM((requests, head_cols + LANES), F32),
                pltpu.SemaphoreType.DMA((5 + pieces,)),
            ],
            grant=12,
            section=0,
            name="heads_0",
        )

    def heads_of(x, tag):
        return run(
            functools.partial(heads_kernel, mems),
            [((slots, head_cols + LANES), F32)] * mems,
            [x, attn_gain, perm, w_query[0], w_key[0], w_value[0]],
            scratch=[pltpu.VMEM((requests, head_cols + LANES), F32)],
            section=int(tag[1:]),
            name="heads" + tag,
        )

    def window(value, after):
        def kernel(value_ref, after_ref, out_ref):
            out_ref[...] = value_ref[...]

        return run(kernel, (value.shape, value.dtype), [value, after], name="window")

    def layer(x, heads, tag):
        attended = run(
            functools.partial(attention_kernel, mems, width, kv_heads),
            ((slots, query_cols), BF16),
            [
                wide_lengths,
                window(cosine, heads[0]) if tag == "_0" else cosine,
                sine,
                heads[0],
                *partners(heads, "mem")[::-1],
                key_cache[0],
                value_cache[0],
            ],
            scratch=[
                pltpu.VMEM((slots, -(-head_cols // HD // 8) * 8, HD), F32),
                pltpu.VMEM((slots, query_cols // HD, key_cache.shape[2]), F32),
                pltpu.VMEM((slots, query_cols), F32),
            ],
            grant=3,
            section=int(tag[1:]),
            name="attention" + tag,
        )
        projected = run(
            functools.partial(project_kernel, mems),
            ((requests, local_width), BF16),
            [perm_back, w_out[0], attended, *partners([attended] * mems, "mem")],
            scratch=[pltpu.VMEM((requests, query_cols), F32)],
            section=int(tag[1:]),
            name="project" + tag,
        )
        after, terms = run(
            functools.partial(hidden_terms_kernel, tps),
            [((requests, local_width), BF16), ((requests, term_cols), BF16)],
            [x, ffn_gain, w_gate[0], w_up[0], projected, *partners([projected] * tps, "tp")],
            section=int(tag[1:]),
            name="terms" + tag,
        )
        down = run(
            functools.partial(down_kernel, mems, width),
            ((requests, local_width), BF16),
            [w_down[0], terms, *partners([terms] * mems, "mem")],
            scratch=[pltpu.VMEM((requests, units), BF16)],
            keep=[window(cosine, terms)] if tag == "_1" else (),
            section=int(tag[1:]),
            name="down" + tag,
        )
        return after, [down, *partners([down] * tps, "tp")]

    after, downs = layer(hidden_in, first_heads(), "_0")
    first = run(
        functools.partial(finish_kernel, tps),
        ((requests, local_width), BF16),
        [after, *downs],
        name="finish",
    )
    sections = lax.axis_size("section")
    passed = lax.ppermute(first, "section", [(i, (i + 1) % sections) for i in range(sections)])
    after, downs = layer(passed, heads_of(passed, "_1"), "_1")
    result = run(
        functools.partial(choose_kernel, tps),
        ((requests, local_width), BF16),
        [after, first, *downs],
        name="choose",
    )
    return result[None]


def solution(mesh):
    placed = (
        P(None, "mem"),
        P(),
        P(),
        P("section", "mem"),
        P("section", "mem", "tp"),
        P("section", "mem", "tp"),
        P("section", "mem", "tp"),
        P("section", "tp", "mem"),
        P("section", "mem"),
        P("section", "mem", "tp"),
        P("section", "mem", "tp"),
        P("section", "tp", "mem"),
        P("section", "mem", None, "tp"),
        P("section", "mem", None, "tp"),
    )
    return jax.shard_map(
        per_device, mesh=mesh, in_specs=placed, out_specs=P("section", None, "mem"), check_vma=False
    )
```

```python
import functools
import math

import jax
import jax.numpy as jnp
from jax import lax
from jax.experimental import pallas as pl
from jax.experimental.pallas import tpu as pltpu
from jax.sharding import PartitionSpec as P

HD = 128
EPSILON = 1e-05
ROPE_BASE = 500000.0
LANES = 128
F32 = jnp.float32
BF16 = jnp.bfloat16
IN_VMEM = pl.BlockSpec(memory_space=pltpu.VMEM)
MIB = 1 << 20


STAGE_US = dict.fromkeys(("heads", "attention", "project", "terms", "down", "window"), 20)


def run(kernel, outs, args, specs=None, scratch=(), grant=2, name=None, keep=(), section=None):
    single = isinstance(outs, tuple)
    out_list = [outs] if single else list(outs)
    flops = STAGE_US.get(name.split("_")[0], 0) * 1150000000
    args, held = list(args), len(args)
    first_out = held + len(keep)

    def in_section(*refs):
        def work():
            kernel(*refs[:held], *refs[first_out:])

        if section is None:
            return work()
        here = lax.axis_index("section") == section
        pl.when(here)(work)

        @pl.when(jnp.logical_not(here))
        def _():
            for out_ref in refs[first_out : first_out + len(out_list)]:
                out_ref[...] = jnp.zeros_like(out_ref)

    result = pl.pallas_call(
        in_section,
        out_shape=[jax.ShapeDtypeStruct(shape, dtype) for shape, dtype in out_list],
        in_specs=(specs or [IN_VMEM] * held) + [IN_VMEM] * len(keep),
        out_specs=[IN_VMEM] * len(out_list),
        scratch_shapes=list(scratch),
        compiler_params=pltpu.CompilerParams(vmem_limit_bytes=grant * MIB),
        cost_estimate=pl.CostEstimate(flops=flops, bytes_accessed=0, transcendentals=0),
        name=name,
    )(*args, *keep)
    return result[0] if single else result


def partners(values, axis, active):
    axes = ("section", "tp", "mem")
    sections, tps, mems = (lax.axis_size(name) for name in axes)

    def pairs(s):
        for section in range(sections):
            for tp in range(tps):
                for mem in range(mems):
                    if section == active:
                        there = (tp ^ s, mem) if axis == "tp" else (tp, mem ^ s)
                    else:
                        there = (tp, mem ^ 1) if axis == "tp" else (tp ^ 1, mem)
                    yield (
                        (section * tps + tp) * mems + mem,
                        (section * tps + there[0]) * mems + there[1],
                    )

    return [
        lax.ppermute(values[s], axes, list(pairs(s))) for s in range(1, lax.axis_size(axis))
    ]


def across(value, s=0):
    axes = ("section", "tp", "mem")
    sections, tps, mems = (lax.axis_size(name) for name in axes)
    pairs = [
        ((section * tps + tp) * mems + mem, ((section ^ 1) * tps + (tp ^ s)) * mems + mem)
        for section in range(sections)
        for tp in range(tps)
        for mem in range(mems)
    ]
    return lax.ppermute(value, axes, pairs)


def tree_sum(pieces):
    while len(pieces) > 1:
        pieces = [a + b for a, b in zip(pieces[::2], pieces[1::2])]
    return pieces[0]


def matmul_into(out_ref, start, rows, weight_ref, step):
    cols = weight_ref.shape[1]
    for at in range(0, cols, step):
        end = min(at + step, cols)
        out_ref[:, start + at : start + end] = jnp.dot(
            rows, weight_ref[:, at:end], preferred_element_type=F32
        ).astype(out_ref.dtype)


def total_of(refs, rows=slice(None), cols=slice(None)):
    return tree_sum([ref[rows, cols].astype(F32) for ref in refs])


def heads_kernel(count, pieces, after_ref, gain_ref, perm_ref, wq_ref, wk_ref, wv_ref, *rest):
    out_refs, x_ref, sums = rest[pieces : pieces + count], *rest[pieces + count :]
    slots = after_ref.shape[0] // count
    x_ref[...] = (after_ref[...].astype(F32) + total_of(rest[:pieces])).astype(BF16)
    x = jnp.dot(perm_ref[...], x_ref[...], preferred_element_type=F32)
    scaled = (x * gain_ref[...].astype(F32)).astype(BF16)
    squares = jnp.sum(x * x, axis=1, keepdims=True)
    at = 0
    for weight_ref in (wq_ref, wk_ref, wv_ref):
        matmul_into(sums, at, scaled, weight_ref, 512)
        at += weight_ref.shape[1]
    sums[:, at:] = jnp.broadcast_to(squares, (x.shape[0], LANES))
    for s in range(count):
        out_refs[s][...] = sums[s * slots : (s + 1) * slots, :]


def first_heads_kernel(count, pieces, x_any, gain_any, owner_any, wq_any, wk_any, wv_any, *rest):
    out_refs = rest[:count]
    x_ref, gain_ref, owner, wq_ref, wk_ref, wv_ref, sums, sems = rest[count:]
    depth, query_cols = wq_ref.shape
    kv_cols = wk_ref.shape[1]
    rows = depth // pieces
    small = [
        pltpu.make_async_copy(source, target, sems.at[i])
        for i, (source, target) in enumerate(
            ((x_any, x_ref), (gain_any, gain_ref), (owner_any, owner), (wk_any, wk_ref), (wv_any, wv_ref))
        )
    ]
    large = [
        pltpu.make_async_copy(
            wq_any.at[p * rows : (p + 1) * rows], wq_ref.at[p * rows : (p + 1) * rows], sems.at[5 + p]
        )
        for p in range(pieces)
    ]
    for copy in small[:3] + large + small[3:]:
        copy.start()
    for copy in small[:3]:
        copy.wait()
    x = x_ref[...].astype(F32)
    scaled = (x * gain_ref[...].astype(F32)).astype(BF16)
    squares = jnp.sum(x * x, axis=1, keepdims=True)
    end = query_cols + 2 * kv_cols
    sums[:, end:] = jnp.broadcast_to(squares, (x.shape[0], LANES))
    for p in range(pieces):
        large[p].wait()
        part = jnp.dot(
            scaled[:, p * rows : (p + 1) * rows],
            wq_ref[p * rows : (p + 1) * rows, :],
            preferred_element_type=F32,
        )
        sums[:, :query_cols] = part if p == 0 else sums[:, :query_cols] + part
    for copy, weight_ref, at in ((small[3], wk_ref, query_cols), (small[4], wv_ref, query_cols + kv_cols)):
        copy.wait()
        matmul_into(sums, at, scaled, weight_ref, 512)
    slots = x.shape[0] // count
    me = lax.axis_index("mem")
    for s in range(count):
        for k in range(slots):
            request = owner[(me ^ s) * slots + k]
            out_refs[s][k : k + 1, :] = sums[pl.ds(request, 1), :]


def attention_kernel(count, width, kv_heads, lengths_ref, cos_ref, sin_ref, *rest):
    pieces = [rest[0], *rest[count - 1 : 0 : -1]]
    key_ref, value_ref = rest[count : count + 2]
    out_ref, head_scr, score_scr, row_scr = rest[count + 2 :]
    slots, context = key_ref.shape[:2]
    query_heads = out_ref.shape[1] // HD
    group = query_heads // kv_heads
    chunk = min(1024, context)
    total = total_of(pieces)
    wide = total.shape[1]
    squares = total[:, wide - LANES : wide - LANES + 1]
    total = total[:, : wide - LANES] * lax.rsqrt(squares / width + EPSILON)
    all_heads = query_heads + 2 * kv_heads
    scale = 1.0 / math.sqrt(HD)
    lane = lax.broadcasted_iota(jnp.int32, (1, HD), 1)
    head_of = lax.broadcasted_iota(jnp.int32, (query_heads, 1), 0) // group
    for s in range(slots):
        for h in range(all_heads):
            head_scr[s, h : h + 1, :] = total[s : s + 1, h * HD : (h + 1) * HD]
    spreads, own_scores, new_values, peaks = [], [], [], []
    for s in range(slots):
        rotating = head_scr[s, : query_heads + kv_heads, :]
        rolled = pltpu.roll(rotating, HD // 2, 1)
        turned = jnp.where(lane < HD // 2, -rolled, rolled)
        rotated = (rotating * cos_ref[s : s + 1, :] + turned * sin_ref[s : s + 1, :]).astype(BF16)
        rotated = rotated.astype(F32)
        queries = rotated[:query_heads]
        new_key = jnp.zeros_like(queries)
        new_value = jnp.zeros_like(queries)
        spread = []
        for g in range(kv_heads):
            mine = head_of == g
            new_key = jnp.where(mine, rotated[query_heads + g : query_heads + g + 1], new_key)
            value_row = query_heads + kv_heads + g
            new_value = jnp.where(mine, head_scr[s, value_row : value_row + 1, :], new_value)
            spread.append(jnp.where(mine, queries, 0.0))
        spreads.append(jnp.concatenate(spread, axis=1).astype(BF16))
        own_scores.append(jnp.sum(queries * new_key, axis=1, keepdims=True) * scale)
        new_values.append(new_value.astype(BF16).astype(F32))
        peaks.append(jnp.full((query_heads, LANES), -jnp.inf, F32))
    position = lax.broadcasted_iota(jnp.int32, (1, chunk), 1)
    for at in range(0, context, chunk):
        for s in range(slots):
            scores = lax.dot_general(
                spreads[s],
                key_ref[s, at : at + chunk, :],
                (((1,), (1,)), ((), ())),
                preferred_element_type=F32,
            )
            scores = jnp.where(position + at < lengths_ref[s : s + 1, :1], scores * scale, -jnp.inf)
            score_scr[s, :, at : at + chunk] = scores
            for i in range(0, chunk, LANES):
                peaks[s] = jnp.maximum(peaks[s], scores[:, i : i + LANES])
    owns, sums, mixes = [], [], []
    for s in range(slots):
        peaks[s] = jnp.maximum(jnp.max(peaks[s], axis=1, keepdims=True), own_scores[s])
        owns.append(jnp.exp(own_scores[s] - peaks[s]))
        sums.append(jnp.zeros((query_heads, LANES), F32))
        mixes.append(jnp.zeros((query_heads, kv_heads * HD), F32))
    for at in range(0, context, chunk):
        for s in range(slots):
            soft = jnp.exp(score_scr[s, :, at : at + chunk] - peaks[s])
            for i in range(0, chunk, LANES):
                sums[s] = sums[s] + soft[:, i : i + LANES]
            mixes[s] = mixes[s] + jnp.dot(
                soft.astype(BF16), value_ref[s, at : at + chunk, :], preferred_element_type=F32
            )
    for s in range(slots):
        picked = jnp.zeros((query_heads, HD), F32)
        for g in range(kv_heads):
            picked = jnp.where(head_of == g, mixes[s][:, g * HD : (g + 1) * HD], picked)
        picked = picked + owns[s].astype(BF16).astype(F32) * new_values[s]
        total_weight = jnp.sum(sums[s], axis=1, keepdims=True) + owns[s]
        head_scr[s, :query_heads, :] = picked / total_weight
    for s in range(slots):
        for h in range(query_heads):
            row_scr[s : s + 1, h * HD : (h + 1) * HD] = head_scr[s, h : h + 1, :]
    out_ref[...] = row_scr[...].astype(BF16)


def project_kernel(count, perm_ref, w_ref, *rest):
    pieces = rest[:count]
    out_ref, rows_scr = rest[count:]
    slots = pieces[0].shape[0]
    for s in range(count):
        rows_scr[s * slots : (s + 1) * slots, :] = pieces[s][...].astype(F32)
    rows = jnp.dot(
        perm_ref[...], rows_scr[...].astype(BF16), preferred_element_type=F32
    ).astype(BF16)
    matmul_into(out_ref, 0, rows, w_ref, 512)


def hidden_terms_kernel(count, x_ref, gain_ref, wg_ref, wu_ref, *rest):
    pieces = rest[:count]
    after_ref, out_ref = rest[count:]
    after = (x_ref[...].astype(F32) + total_of(pieces)).astype(BF16)
    after_ref[...] = after
    after = after.astype(F32)
    scaled = (after * gain_ref[...].astype(F32)).astype(BF16)
    squares = jnp.broadcast_to(
        jnp.sum(after * after, axis=1, keepdims=True), (after.shape[0], LANES)
    )
    matmul_into(out_ref, 0, scaled, wg_ref, 512)
    matmul_into(out_ref, wg_ref.shape[1], scaled, wu_ref, 512)
    at = wg_ref.shape[1] + wu_ref.shape[1]
    for _ in range(3):
        part = squares.astype(BF16)
        out_ref[:, at : at + LANES] = part
        squares = squares - part.astype(F32)
        at += LANES


def down_kernel(count, width, w_ref, *rest):
    pieces = rest[:count]
    out_ref, hidden_scr = rest[count:]
    units = w_ref.shape[0]
    squares = tree_sum(
        [
            (
                ref[:, 2 * units : 2 * units + LANES].astype(F32)
                + ref[:, 2 * units + LANES : 2 * units + 2 * LANES].astype(F32)
            )
            + ref[:, 2 * units + 2 * LANES :].astype(F32)
            for ref in pieces
        ]
    )
    factor = lax.rsqrt(squares[:, :1] / width + EPSILON)
    step = 512
    while units % step:
        step //= 2
    for at in range(0, units, step):
        gate = total_of(pieces, cols=slice(at, at + step)) * factor
        up = total_of(pieces, cols=slice(units + at, units + at + step)) * factor
        hidden_scr[:, at : at + step] = (gate / (1.0 + jnp.exp(-gate)) * up).astype(BF16)
    matmul_into(out_ref, 0, hidden_scr[...], w_ref, 512)


def choose_kernel(count, x_ref, first_ref, *rest):
    pieces = rest[:count]
    out_ref = rest[count]
    second = (x_ref[...].astype(F32) + total_of(pieces)).astype(BF16).astype(F32)
    first = first_ref[...].astype(F32)
    out_ref[...] = jnp.where(lax.axis_index("section") == 0, first, second).astype(BF16)


def per_device(
    hidden_in,
    lengths,
    owner_order,
    attn_gain,
    w_query,
    w_key,
    w_value,
    w_out,
    ffn_gain,
    w_gate,
    w_up,
    w_down,
    key_cache,
    value_cache,
):
    mems, tps = lax.axis_size("mem"), lax.axis_size("tp")
    requests, local_width = hidden_in.shape
    slots = requests // mems
    width = local_width * mems
    query_cols, kv_cols, units = w_query.shape[2], w_key.shape[2], w_gate.shape[2]
    kv_heads = kv_cols // HD
    me = lax.axis_index("mem")

    group = jnp.arange(requests, dtype=jnp.int32) // slots
    slot_index = (group ^ me) * slots + jnp.arange(requests, dtype=jnp.int32) % slots
    every = jnp.arange(requests, dtype=jnp.int32)
    request_of = jnp.sum(
        jnp.where(slot_index[:, None] == every[None, :], owner_order[None, :], 0), axis=1
    )
    here = request_of[:, None] == every[None, :]
    perm = here.astype(BF16)
    perm_back = (request_of[None, :] == every[:, None]).astype(BF16)
    slot_lengths = jnp.sum(jnp.where(here[:slots], lengths[None, :], 0), axis=1)
    wide_lengths = jnp.broadcast_to(slot_lengths[:, None], (slots, LANES))
    freqs = ROPE_BASE ** (-(jnp.arange(HD // 2, dtype=F32) * 2.0) / HD)
    angles = slot_lengths.astype(F32)[:, None] * freqs[None, :]
    cosine = jnp.concatenate([jnp.cos(angles)] * 2, axis=-1)
    sine = jnp.concatenate([jnp.sin(angles)] * 2, axis=-1)

    head_cols = query_cols + 2 * kv_cols
    term_cols = 2 * units + 3 * LANES

    def first_heads():
        pieces = 8
        return run(
            functools.partial(first_heads_kernel, mems, pieces),
            [((slots, head_cols + LANES), F32)] * mems,
            [
                pltpu.with_memory_space_constraint(source, pltpu.HBM)
                for source in (hidden_in, attn_gain, owner_order, w_query[0], w_key[0], w_value[0])
            ],
            specs=[pl.BlockSpec(memory_space=pltpu.HBM)] * 6,
            scratch=[
                pltpu.VMEM((requests, local_width), BF16),
                pltpu.VMEM((1, local_width), BF16),
                pltpu.SMEM((requests,), jnp.int32),
                pltpu.VMEM((local_width, query_cols), BF16),
                pltpu.VMEM((local_width, kv_cols), BF16),
                pltpu.VMEM((local_width, kv_cols), BF16),
                pltpu.VMEM((requests, head_cols + LANES), F32),
                pltpu.SemaphoreType.DMA((5 + pieces,)),
            ],
            grant=12,
            section=0,
            name="heads_0",
        )

    def second_heads(after, downs):
        *heads, x = run(
            functools.partial(heads_kernel, mems, len(downs)),
            [((slots, head_cols + LANES), F32)] * mems + [((requests, local_width), BF16)],
            [after, attn_gain, perm, w_query[0], w_key[0], w_value[0], *downs],
            scratch=[pltpu.VMEM((requests, head_cols + LANES), F32)],
            section=1,
            name="heads_1",
        )
        return x, heads

    def window(value, after):
        def kernel(value_ref, after_ref, out_ref):
            out_ref[...] = value_ref[...]

        return run(kernel, (value.shape, value.dtype), [value, after], name="window")

    def layer(x, heads, tag):
        attended = run(
            functools.partial(attention_kernel, mems, width, kv_heads),
            ((slots, query_cols), BF16),
            [
                wide_lengths,
                window(cosine, heads[0]) if tag == "_0" else cosine,
                sine,
                heads[0],
                *partners(heads, "mem", int(tag[1:]))[::-1],
                key_cache[0],
                value_cache[0],
            ],
            scratch=[
                pltpu.VMEM((slots, -(-head_cols // HD // 8) * 8, HD), F32),
                pltpu.VMEM((slots, query_cols // HD, key_cache.shape[2]), F32),
                pltpu.VMEM((slots, query_cols), F32),
            ],
            grant=3,
            section=int(tag[1:]),
            name="attention" + tag,
        )
        projected = run(
            functools.partial(project_kernel, mems),
            ((requests, local_width), BF16),
            [perm_back, w_out[0], attended, *partners([attended] * mems, "mem", int(tag[1:]))],
            scratch=[pltpu.VMEM((requests, query_cols), F32)],
            section=int(tag[1:]),
            name="project" + tag,
        )
        after, terms = run(
            functools.partial(hidden_terms_kernel, tps),
            [((requests, local_width), BF16), ((requests, term_cols), BF16)],
            [x, ffn_gain, w_gate[0], w_up[0], projected, *partners([projected] * tps, "tp", int(tag[1:]))],
            section=int(tag[1:]),
            name="terms" + tag,
        )
        down = run(
            functools.partial(down_kernel, mems, width),
            ((requests, local_width), BF16),
            [w_down[0], terms, *partners([terms] * mems, "mem", int(tag[1:]))],
            scratch=[pltpu.VMEM((requests, units), BF16)],
            keep=[window(cosine, terms)] if tag == "_1" else (),
            section=int(tag[1:]),
            name="down" + tag,
        )
        return after, down

    after, down = layer(hidden_in, first_heads(), "_0")
    downs = [across(down, s) for s in range(tps)]
    passed, heads = second_heads(across(after), downs)
    first = across(passed)
    after, down = layer(passed, heads, "_1")
    result = run(
        functools.partial(choose_kernel, tps),
        ((requests, local_width), BF16),
        [after, first, down, *partners([down] * tps, "tp", 1)],
        name="choose",
    )
    return result[None]


def solution(mesh):
    placed = (
        P(None, "mem"),
        P(),
        P(),
        P("section", "mem"),
        P("section", "mem", "tp"),
        P("section", "mem", "tp"),
        P("section", "mem", "tp"),
        P("section", "tp", "mem"),
        P("section", "mem"),
        P("section", "mem", "tp"),
        P("section", "mem", "tp"),
        P("section", "tp", "mem"),
        P("section", "mem", None, "tp"),
        P("section", "mem", None, "tp"),
    )
    return jax.shard_map(
        per_device, mesh=mesh, in_specs=placed, out_specs=P("section", None, "mem"), check_vma=False
    )
```

```python
import functools
import math

import jax
import jax.numpy as jnp
from jax import lax
from jax.experimental import pallas as pl
from jax.experimental.pallas import tpu as pltpu
from jax.sharding import PartitionSpec as P

HD = 128
EPSILON = 1e-05
ROPE_BASE = 500000.0
LANES = 128
F32 = jnp.float32
BF16 = jnp.bfloat16
IN_VMEM = pl.BlockSpec(memory_space=pltpu.VMEM)
MIB = 1 << 20


STAGE_US = dict.fromkeys(("heads", "attention", "project", "terms", "down", "window"), 20)


def run(kernel, outs, args, specs=None, scratch=(), grant=2, name=None, keep=(), section=None):
    single = isinstance(outs, tuple)
    out_list = [outs] if single else list(outs)
    flops = STAGE_US.get(name.split("_")[0], 0) * 1150000000
    args, held = list(args), len(args)
    first_out = held + len(keep)

    def in_section(*refs):
        def work():
            kernel(*refs[:held], *refs[first_out:])

        if section is None:
            return work()
        here = lax.axis_index("section") == section
        pl.when(here)(work)

        @pl.when(jnp.logical_not(here))
        def _():
            for out_ref in refs[first_out : first_out + len(out_list)]:
                out_ref[...] = jnp.zeros_like(out_ref)

    result = pl.pallas_call(
        in_section,
        out_shape=[jax.ShapeDtypeStruct(shape, dtype) for shape, dtype in out_list],
        in_specs=(specs or [IN_VMEM] * held) + [IN_VMEM] * len(keep),
        out_specs=[IN_VMEM] * len(out_list),
        scratch_shapes=list(scratch),
        compiler_params=pltpu.CompilerParams(vmem_limit_bytes=grant * MIB),
        cost_estimate=pl.CostEstimate(flops=flops, bytes_accessed=0, transcendentals=0),
        name=name,
    )(*args, *keep)
    return result[0] if single else result


def partners(values, axis, active):
    axes = ("section", "tp", "mem")
    sections, tps, mems = (lax.axis_size(name) for name in axes)

    def pairs(s):
        for section in range(sections):
            for tp in range(tps):
                for mem in range(mems):
                    if section == active:
                        there = (tp ^ s, mem) if axis == "tp" else (tp, mem ^ s)
                    else:
                        there = (tp, mem ^ 1) if axis == "tp" else (tp ^ 1, mem)
                    yield (
                        (section * tps + tp) * mems + mem,
                        (section * tps + there[0]) * mems + there[1],
                    )

    return [
        lax.ppermute(values[s], axes, list(pairs(s))) for s in range(1, lax.axis_size(axis))
    ]


def across(value, s=0):
    axes = ("section", "tp", "mem")
    sections, tps, mems = (lax.axis_size(name) for name in axes)
    pairs = [
        ((section * tps + tp) * mems + mem, ((section ^ 1) * tps + (tp ^ s)) * mems + mem)
        for section in range(sections)
        for tp in range(tps)
        for mem in range(mems)
    ]
    return lax.ppermute(value, axes, pairs)


def tp_order(count):
    return (1, 3, 2) if count == 4 else tuple(range(1, count))


def tp_taken(pieces):
    return [pieces[s - 1] for s in tp_order(len(pieces) + 1)]


def tp_sum(refs):
    order = (0, *tp_order(len(refs)))
    return total_of([refs[order.index(s)] for s in range(len(refs))])


def tree_sum(pieces):
    while len(pieces) > 1:
        pieces = [a + b for a, b in zip(pieces[::2], pieces[1::2])]
    return pieces[0]


def matmul_into(out_ref, start, rows, weight_ref, step):
    cols = weight_ref.shape[1]
    for at in range(0, cols, step):
        end = min(at + step, cols)
        out_ref[:, start + at : start + end] = jnp.dot(
            rows, weight_ref[:, at:end], preferred_element_type=F32
        ).astype(out_ref.dtype)


def total_of(refs, rows=slice(None), cols=slice(None)):
    return tree_sum([ref[rows, cols].astype(F32) for ref in refs])


def heads_kernel(count, pieces, after_ref, gain_ref, perm_ref, wq_ref, wk_ref, wv_ref, *rest):
    out_refs, x_ref, sums = rest[pieces : pieces + count], *rest[pieces + count :]
    slots = after_ref.shape[0] // count
    x_ref[...] = (after_ref[...].astype(F32) + total_of(rest[:pieces])).astype(BF16)
    x = jnp.dot(perm_ref[...], x_ref[...], preferred_element_type=F32)
    scaled = (x * gain_ref[...].astype(F32)).astype(BF16)
    squares = jnp.sum(x * x, axis=1, keepdims=True)
    at = 0
    for weight_ref in (wq_ref, wk_ref, wv_ref):
        matmul_into(sums, at, scaled, weight_ref, 512)
        at += weight_ref.shape[1]
    sums[:, at:] = jnp.broadcast_to(squares, (x.shape[0], LANES))
    for s in range(count):
        out_refs[s][...] = sums[s * slots : (s + 1) * slots, :]


def first_heads_kernel(count, pieces, x_any, gain_any, owner_any, wq_any, wk_any, wv_any, *rest):
    out_refs = rest[:count]
    x_ref, gain_ref, owner, wq_ref, wk_ref, wv_ref, sums, sems = rest[count:]
    depth, query_cols = wq_ref.shape
    kv_cols = wk_ref.shape[1]
    rows = depth // pieces
    small = [
        pltpu.make_async_copy(source, target, sems.at[i])
        for i, (source, target) in enumerate(
            ((x_any, x_ref), (gain_any, gain_ref), (owner_any, owner), (wk_any, wk_ref), (wv_any, wv_ref))
        )
    ]
    large = [
        pltpu.make_async_copy(
            wq_any.at[p * rows : (p + 1) * rows], wq_ref.at[p * rows : (p + 1) * rows], sems.at[5 + p]
        )
        for p in range(pieces)
    ]
    for copy in small[:3] + large + small[3:]:
        copy.start()
    for copy in small[:3]:
        copy.wait()
    x = x_ref[...].astype(F32)
    scaled = (x * gain_ref[...].astype(F32)).astype(BF16)
    squares = jnp.sum(x * x, axis=1, keepdims=True)
    end = query_cols + 2 * kv_cols
    sums[:, end:] = jnp.broadcast_to(squares, (x.shape[0], LANES))
    for p in range(pieces):
        large[p].wait()
        part = jnp.dot(
            scaled[:, p * rows : (p + 1) * rows],
            wq_ref[p * rows : (p + 1) * rows, :],
            preferred_element_type=F32,
        )
        sums[:, :query_cols] = part if p == 0 else sums[:, :query_cols] + part
    for copy, weight_ref, at in ((small[3], wk_ref, query_cols), (small[4], wv_ref, query_cols + kv_cols)):
        copy.wait()
        matmul_into(sums, at, scaled, weight_ref, 512)
    slots = x.shape[0] // count
    me = lax.axis_index("mem")
    for s in range(count):
        for k in range(slots):
            request = owner[(me ^ s) * slots + k]
            out_refs[s][k : k + 1, :] = sums[pl.ds(request, 1), :]


def attention_kernel(count, width, kv_heads, lengths_ref, cos_ref, sin_ref, *rest):
    pieces = [rest[0], *rest[count - 1 : 0 : -1]]
    key_ref, value_ref = rest[count : count + 2]
    out_ref, head_scr, score_scr, row_scr = rest[count + 2 :]
    slots, context = key_ref.shape[:2]
    query_heads = out_ref.shape[1] // HD
    group = query_heads // kv_heads
    chunk = min(1024, context)
    total = total_of(pieces)
    wide = total.shape[1]
    squares = total[:, wide - LANES : wide - LANES + 1]
    total = total[:, : wide - LANES] * lax.rsqrt(squares / width + EPSILON)
    all_heads = query_heads + 2 * kv_heads
    scale = 1.0 / math.sqrt(HD)
    lane = lax.broadcasted_iota(jnp.int32, (1, HD), 1)
    head_of = lax.broadcasted_iota(jnp.int32, (query_heads, 1), 0) // group
    for s in range(slots):
        for h in range(all_heads):
            head_scr[s, h : h + 1, :] = total[s : s + 1, h * HD : (h + 1) * HD]
    spreads, own_scores, new_values, peaks = [], [], [], []
    for s in range(slots):
        rotating = head_scr[s, : query_heads + kv_heads, :]
        rolled = pltpu.roll(rotating, HD // 2, 1)
        turned = jnp.where(lane < HD // 2, -rolled, rolled)
        rotated = (rotating * cos_ref[s : s + 1, :] + turned * sin_ref[s : s + 1, :]).astype(BF16)
        rotated = rotated.astype(F32)
        queries = rotated[:query_heads]
        new_key = jnp.zeros_like(queries)
        new_value = jnp.zeros_like(queries)
        spread = []
        for g in range(kv_heads):
            mine = head_of == g
            new_key = jnp.where(mine, rotated[query_heads + g : query_heads + g + 1], new_key)
            value_row = query_heads + kv_heads + g
            new_value = jnp.where(mine, head_scr[s, value_row : value_row + 1, :], new_value)
            spread.append(jnp.where(mine, queries, 0.0))
        spreads.append(jnp.concatenate(spread, axis=1).astype(BF16))
        own_scores.append(jnp.sum(queries * new_key, axis=1, keepdims=True) * scale)
        new_values.append(new_value.astype(BF16).astype(F32))
        peaks.append(jnp.full((query_heads, LANES), -jnp.inf, F32))
    position = lax.broadcasted_iota(jnp.int32, (1, chunk), 1)
    for at in range(0, context, chunk):
        for s in range(slots):
            scores = lax.dot_general(
                spreads[s],
                key_ref[s, at : at + chunk, :],
                (((1,), (1,)), ((), ())),
                preferred_element_type=F32,
            )
            scores = jnp.where(position + at < lengths_ref[s : s + 1, :1], scores * scale, -jnp.inf)
            score_scr[s, :, at : at + chunk] = scores
            for i in range(0, chunk, LANES):
                peaks[s] = jnp.maximum(peaks[s], scores[:, i : i + LANES])
    owns, sums, mixes = [], [], []
    for s in range(slots):
        peaks[s] = jnp.maximum(jnp.max(peaks[s], axis=1, keepdims=True), own_scores[s])
        owns.append(jnp.exp(own_scores[s] - peaks[s]))
        sums.append(jnp.zeros((query_heads, LANES), F32))
        mixes.append(jnp.zeros((query_heads, kv_heads * HD), F32))
    for at in range(0, context, chunk):
        for s in range(slots):
            soft = jnp.exp(score_scr[s, :, at : at + chunk] - peaks[s])
            for i in range(0, chunk, LANES):
                sums[s] = sums[s] + soft[:, i : i + LANES]
            mixes[s] = mixes[s] + jnp.dot(
                soft.astype(BF16), value_ref[s, at : at + chunk, :], preferred_element_type=F32
            )
    for s in range(slots):
        picked = jnp.zeros((query_heads, HD), F32)
        for g in range(kv_heads):
            picked = jnp.where(head_of == g, mixes[s][:, g * HD : (g + 1) * HD], picked)
        picked = picked + owns[s].astype(BF16).astype(F32) * new_values[s]
        total_weight = jnp.sum(sums[s], axis=1, keepdims=True) + owns[s]
        head_scr[s, :query_heads, :] = picked / total_weight
    for s in range(slots):
        for h in range(query_heads):
            row_scr[s : s + 1, h * HD : (h + 1) * HD] = head_scr[s, h : h + 1, :]
    out_ref[...] = row_scr[...].astype(BF16)


def project_kernel(count, perm_ref, w_ref, *rest):
    pieces = rest[:count]
    out_ref, rows_scr = rest[count:]
    slots = pieces[0].shape[0]
    for s in range(count):
        rows_scr[s * slots : (s + 1) * slots, :] = pieces[s][...].astype(F32)
    rows = jnp.dot(
        perm_ref[...], rows_scr[...].astype(BF16), preferred_element_type=F32
    ).astype(BF16)
    matmul_into(out_ref, 0, rows, w_ref, 512)


def hidden_terms_kernel(count, x_ref, gain_ref, wg_ref, wu_ref, *rest):
    pieces = rest[:count]
    after_ref, out_ref = rest[count:]
    after = (x_ref[...].astype(F32) + tp_sum(pieces)).astype(BF16)
    after_ref[...] = after
    after = after.astype(F32)
    scaled = (after * gain_ref[...].astype(F32)).astype(BF16)
    squares = jnp.broadcast_to(
        jnp.sum(after * after, axis=1, keepdims=True), (after.shape[0], LANES)
    )
    matmul_into(out_ref, 0, scaled, wg_ref, 512)
    matmul_into(out_ref, wg_ref.shape[1], scaled, wu_ref, 512)
    at = wg_ref.shape[1] + wu_ref.shape[1]
    for _ in range(3):
        part = squares.astype(BF16)
        out_ref[:, at : at + LANES] = part
        squares = squares - part.astype(F32)
        at += LANES


def down_kernel(count, width, w_ref, *rest):
    pieces = rest[:count]
    out_ref, hidden_scr = rest[count:]
    units = w_ref.shape[0]
    squares = tree_sum(
        [
            (
                ref[:, 2 * units : 2 * units + LANES].astype(F32)
                + ref[:, 2 * units + LANES : 2 * units + 2 * LANES].astype(F32)
            )
            + ref[:, 2 * units + 2 * LANES :].astype(F32)
            for ref in pieces
        ]
    )
    factor = lax.rsqrt(squares[:, :1] / width + EPSILON)
    step = 512
    while units % step:
        step //= 2
    for at in range(0, units, step):
        gate = total_of(pieces, cols=slice(at, at + step)) * factor
        up = total_of(pieces, cols=slice(units + at, units + at + step)) * factor
        hidden_scr[:, at : at + step] = (gate / (1.0 + jnp.exp(-gate)) * up).astype(BF16)
    matmul_into(out_ref, 0, hidden_scr[...], w_ref, 512)


def choose_kernel(count, x_ref, first_ref, *rest):
    pieces = rest[:count]
    out_ref = rest[count]
    second = (x_ref[...].astype(F32) + tp_sum(pieces)).astype(BF16).astype(F32)
    first = first_ref[...].astype(F32)
    out_ref[...] = jnp.where(lax.axis_index("section") == 0, first, second).astype(BF16)


def per_device(
    hidden_in,
    lengths,
    owner_order,
    attn_gain,
    w_query,
    w_key,
    w_value,
    w_out,
    ffn_gain,
    w_gate,
    w_up,
    w_down,
    key_cache,
    value_cache,
):
    mems, tps = lax.axis_size("mem"), lax.axis_size("tp")
    requests, local_width = hidden_in.shape
    slots = requests // mems
    width = local_width * mems
    query_cols, kv_cols, units = w_query.shape[2], w_key.shape[2], w_gate.shape[2]
    kv_heads = kv_cols // HD
    me = lax.axis_index("mem")

    group = jnp.arange(requests, dtype=jnp.int32) // slots
    slot_index = (group ^ me) * slots + jnp.arange(requests, dtype=jnp.int32) % slots
    every = jnp.arange(requests, dtype=jnp.int32)
    request_of = jnp.sum(
        jnp.where(slot_index[:, None] == every[None, :], owner_order[None, :], 0), axis=1
    )
    here = request_of[:, None] == every[None, :]
    perm = here.astype(BF16)
    perm_back = (request_of[None, :] == every[:, None]).astype(BF16)
    slot_lengths = jnp.sum(jnp.where(here[:slots], lengths[None, :], 0), axis=1)
    wide_lengths = jnp.broadcast_to(slot_lengths[:, None], (slots, LANES))
    freqs = ROPE_BASE ** (-(jnp.arange(HD // 2, dtype=F32) * 2.0) / HD)
    angles = slot_lengths.astype(F32)[:, None] * freqs[None, :]
    cosine = jnp.concatenate([jnp.cos(angles)] * 2, axis=-1)
    sine = jnp.concatenate([jnp.sin(angles)] * 2, axis=-1)

    head_cols = query_cols + 2 * kv_cols
    term_cols = 2 * units + 3 * LANES

    def first_heads():
        pieces = 8
        return run(
            functools.partial(first_heads_kernel, mems, pieces),
            [((slots, head_cols + LANES), F32)] * mems,
            [
                pltpu.with_memory_space_constraint(source, pltpu.HBM)
                for source in (hidden_in, attn_gain, owner_order, w_query[0], w_key[0], w_value[0])
            ],
            specs=[pl.BlockSpec(memory_space=pltpu.HBM)] * 6,
            scratch=[
                pltpu.VMEM((requests, local_width), BF16),
                pltpu.VMEM((1, local_width), BF16),
                pltpu.SMEM((requests,), jnp.int32),
                pltpu.VMEM((local_width, query_cols), BF16),
                pltpu.VMEM((local_width, kv_cols), BF16),
                pltpu.VMEM((local_width, kv_cols), BF16),
                pltpu.VMEM((requests, head_cols + LANES), F32),
                pltpu.SemaphoreType.DMA((5 + pieces,)),
            ],
            grant=12,
            section=0,
            name="heads_0",
        )

    def second_heads(after, downs):
        *heads, x = run(
            functools.partial(heads_kernel, mems, len(downs)),
            [((slots, head_cols + LANES), F32)] * mems + [((requests, local_width), BF16)],
            [after, attn_gain, perm, w_query[0], w_key[0], w_value[0], *downs],
            scratch=[pltpu.VMEM((requests, head_cols + LANES), F32)],
            section=1,
            name="heads_1",
        )
        return x, heads

    def window(value, after):
        def kernel(value_ref, after_ref, out_ref):
            out_ref[...] = value_ref[...]

        return run(kernel, (value.shape, value.dtype), [value, after], name="window")

    def layer(x, heads, tag):
        attended = run(
            functools.partial(attention_kernel, mems, width, kv_heads),
            ((slots, query_cols), BF16),
            [
                wide_lengths,
                window(cosine, heads[0]) if tag == "_0" else cosine,
                sine,
                heads[0],
                *partners(heads, "mem", int(tag[1:]))[::-1],
                key_cache[0],
                value_cache[0],
            ],
            scratch=[
                pltpu.VMEM((slots, -(-head_cols // HD // 8) * 8, HD), F32),
                pltpu.VMEM((slots, query_cols // HD, key_cache.shape[2]), F32),
                pltpu.VMEM((slots, query_cols), F32),
            ],
            grant=3,
            section=int(tag[1:]),
            name="attention" + tag,
        )
        projected = run(
            functools.partial(project_kernel, mems),
            ((requests, local_width), BF16),
            [perm_back, w_out[0], attended, *partners([attended] * mems, "mem", int(tag[1:]))],
            scratch=[pltpu.VMEM((requests, query_cols), F32)],
            section=int(tag[1:]),
            name="project" + tag,
        )
        after, terms = run(
            functools.partial(hidden_terms_kernel, tps),
            [((requests, local_width), BF16), ((requests, term_cols), BF16)],
            [x, ffn_gain, w_gate[0], w_up[0], projected, *tp_taken(partners([projected] * tps, "tp", int(tag[1:])))],
            section=int(tag[1:]),
            name="terms" + tag,
        )
        down = run(
            functools.partial(down_kernel, mems, width),
            ((requests, local_width), BF16),
            [w_down[0], terms, *partners([terms] * mems, "mem", int(tag[1:]))],
            scratch=[pltpu.VMEM((requests, units), BF16)],
            keep=[window(cosine, terms)] if tag == "_1" else (),
            section=int(tag[1:]),
            name="down" + tag,
        )
        return after, down

    after, down = layer(hidden_in, first_heads(), "_0")
    downs = [across(down, s) for s in range(tps)]
    passed, heads = second_heads(across(after), downs)
    first = across(passed)
    after, down = layer(passed, heads, "_1")
    result = run(
        functools.partial(choose_kernel, tps),
        ((requests, local_width), BF16),
        [after, first, down, *tp_taken(partners([down] * tps, "tp", 1))],
        name="choose",
    )
    return result[None]


def solution(mesh):
    placed = (
        P(None, "mem"),
        P(),
        P(),
        P("section", "mem"),
        P("section", "mem", "tp"),
        P("section", "mem", "tp"),
        P("section", "mem", "tp"),
        P("section", "tp", "mem"),
        P("section", "mem"),
        P("section", "mem", "tp"),
        P("section", "mem", "tp"),
        P("section", "tp", "mem"),
        P("section", "mem", None, "tp"),
        P("section", "mem", None, "tp"),
    )
    return jax.shard_map(
        per_device, mesh=mesh, in_specs=placed, out_specs=P("section", None, "mem"), check_vma=False
    )
```
